128 devices in a mesh: tx: 16 (over x, y), ty: 8 (over z, core).
Axes of the slice: x: 4, y: 4, z: 4, core: 2. Of those that a mesh axis runs over, the one named last changes fastest.
Arguments:
- mag: float32 [3, 2048, 2048], P(None, 'tx', 'ty'), may hold values from -1 to 1, as said below
- occupancy: int32 [2048, 2048], P('tx', 'ty'), may hold values from 0 to 1
- kernel_spectrum: float32 [4, 4096, 4096], P(None, ('tx', 'ty')), may hold values from -0.5 to 1, as said below
Outputs:
- mag_next: float32 [3, 2048, 2048], P(None, 'tx', 'ty')
- mean_rate: float32 [3, 2048, 2048], P(None, 'tx', 'ty')
The draws below stay inside these ranges and needn't reach their ends.
Inputs may be any that keep to these rules, and one draw needn't show every extreme that they name: `mag`: each cell's three components have unit length. `kernel_spectrum`: each component is unchanged under (y frequency, x frequency) -> ((4096 - y frequency) mod 2 * 2048, (4096 - x frequency) mod 2 * 2048).
All inputs are finite; a program needn't handle non-finite values.
Results may differ from the reference program's by a relative error of at most 0.00005.
Values sent between devices are 32-bit elements; how exact they have to be, the bound alone decides.
A program may use at most 192 MiB of HBM per device.

```python
import jax
import jax.numpy as jnp
from jax import lax

NX = 2048
NY = 2048
N_TX = 16
N_TY = 8


def draw_mag(key, part):
    raw = jax.random.normal(key, (3, NX, NY), jnp.float32)
    return raw / jnp.sqrt(jnp.sum(raw * raw, axis=0, keepdims=True) + 1e-12)


def draw_occupancy(key, part):
    block_key, cell_key = jax.random.split(jax.random.fold_in(key, 7))
    block_rows = NX // 8
    block_cols = NY // 8
    levels = jax.random.randint(block_key, (block_rows, block_cols), 0, 8)
    limits = 5 + 3 * jnp.arange(block_rows, dtype=jnp.int32) // max(block_rows - 1, 1)
    blocks = (levels < limits[:, None]).astype(jnp.int32)
    cells = (jax.random.randint(cell_key, (NX, NY), 0, 8) != 0).astype(jnp.int32)
    pattern = jnp.repeat(jnp.repeat(blocks, 8, axis=0), 8, axis=1) * cells
    row_band = jnp.arange(NX, dtype=jnp.int32) % (NX // N_TX) < 8
    col_band = jnp.arange(NY, dtype=jnp.int32) % (NY // N_TY) < 8
    band = jnp.logical_or(row_band[:, None], col_band[None, :]).astype(jnp.int32)
    return jnp.maximum(pattern, band)


def draw_kernel_spectrum(key, part):
    raw = jax.random.uniform(jax.random.fold_in(key, 11), (4, 2 * NY, 2 * NX), jnp.float32, -0.5, 1.0)
    mirror = jnp.roll(jnp.flip(raw, axis=(1, 2)), 1, axis=(1, 2))
    return 0.5 * (raw + mirror)


def setup_inputs(seed: int = 0) -> dict:
    key_list = jax.random.split(jax.random.key(seed), 4)
    return {
        "mag": draw_mag(jax.random.fold_in(key_list[3], 71), 0),
        "occupancy": draw_occupancy(jax.random.fold_in(key_list[3], 71), 0),
        "kernel_spectrum": draw_kernel_spectrum(jax.random.fold_in(key_list[3], 71), 0),
    }


DAMPING = 0.3
STIFFNESS = 0.25
TIME_STEP = 0.25

def neighbours(field):
    padded = jnp.pad(field, ((0, 0), (1, 1), (1, 1)))
    return padded[:, 2:, 1:-1] + padded[:, :-2, 1:-1] + padded[:, 1:-1, 2:] + padded[:, 1:-1, :-2]

def cross(left, right):
    return jnp.stack([left[1] * right[2] - left[2] * right[1], left[2] * right[0] - left[0] * right[2], left[0] * right[1] - left[1] * right[0]])

def demag(field, kernel_spectrum):
    padded = jnp.zeros((3, 2 * NX, 2 * NY), field.dtype).at[:, :NX, :NY].set(field)
    spectrum = jnp.fft.fft2(padded)
    kernel = jnp.transpose(kernel_spectrum, (0, 2, 1))
    field_x = -(kernel[0] * spectrum[0] + kernel[3] * spectrum[1])
    field_y = -(kernel[3] * spectrum[0] + kernel[1] * spectrum[1])
    field_z = -(kernel[2] * spectrum[2])
    back = jnp.fft.ifft2(jnp.stack([field_x, field_y, field_z])).real
    return back[:, :NX, :NY].astype(field.dtype)

def reference(mag, occupancy, kernel_spectrum):
    occ = occupancy.astype(jnp.float32)
    start = mag * occ[None]

    def rate(field):
        effective = demag(field, kernel_spectrum) + STIFFNESS * neighbours(field)
        torque = cross(field, effective)
        return -(torque + DAMPING * cross(field, torque)) / (1.0 + DAMPING * DAMPING)

    def normal(vector):
        return vector / jnp.sqrt(lax.optimization_barrier(jnp.sum(vector * vector, axis=0)) + 1.0 - occ)[None]
    first = rate(start)
    middle = normal(start + TIME_STEP * first)
    second = rate(middle)
    second = second - lax.optimization_barrier(jnp.sum(second * start, axis=0))[None] * start
    mean_rate = 0.5 * (first + second)
    mag_next = normal(start + TIME_STEP * mean_rate)
    return (mag_next, mean_rate)
```

```python
import functools
import math

import jax
import jax.numpy as jnp
import ml_dtypes
import numpy as np
from jax import lax
from jax.experimental import pallas as pl
from jax.experimental.pallas import tpu as pltpu
from jax.sharding import PartitionSpec as P

DAMPING = 0.3
STIFFNESS = 0.25
TIME_STEP = 0.25
MESH = pl.DeviceIdType.MESH
F32 = jnp.float32
BF16 = jnp.bfloat16


(T_WA, T_WAQ, T_W1R, T_W1I, T_W2, T_W2I, T_BR, T_BI, T_W3, T_W3Q, T_S2, T_S2I) = (
    0, 1, 2, 3, 4, 5, 6, 7, 8, 9, 10, 13,
)
N_TABLES = 16


def angle(left, right, length):
    product = np.arange(left)[:, None] * np.arange(right)[None, :] % length
    return 2.0 * math.pi * product / length


def matrices():
    out = np.zeros((N_TABLES, 256, 256))
    th = angle(128, 128, 128)
    cos, sin = np.cos(th), np.sin(th)
    out[T_WA] = np.block([[cos, sin], [-sin, cos]])
    scale = -(2.0**-24)
    out[T_W3] = 2.0 * scale * np.block([[cos, sin], [-sin, cos]])
    ph = th + 2.0 * math.pi * np.arange(128)[None, :] / 256.0
    low, high = np.arange(1, 64), np.arange(64, 128)
    sign = 1.0 - 2.0 * (np.arange(128) % 2)
    q = np.zeros((2, 128, 2, 128))
    q[0, 0, 0], q[1, 0, 0] = 1.0, sign
    q[0, low, 0], q[1, low, 0] = cos[low], -sin[low]
    q[0, high, 1], q[1, high, 1] = np.cos(ph)[high], -np.sin(ph)[high]
    out[T_WAQ] = q.reshape(256, 256)
    weight = np.full((128, 1, 1), 2.0)
    weight[0] = 1.0
    out[T_W3Q] = scale * (q * weight).reshape(256, 256)
    th = angle(256, 128, 256)
    cos, sin = np.cos(th), np.sin(th)
    out[T_W1R] = np.concatenate([cos, sin], 1)
    out[T_W1I] = np.concatenate([-sin, cos], 1)
    out[T_BR] = np.concatenate([cos.T, sin.T], 0)
    out[T_BI] = np.concatenate([-sin.T, cos.T], 0)
    th = angle(16, 16, 16)
    cos, sin = np.cos(th), np.sin(th)
    eight = np.eye(8)
    wc = np.einsum("ab,id->aidb", eight, cos).reshape(128, 128)
    ws = np.einsum("ab,id->aidb", eight, sin).reshape(128, 128)
    out[T_W2] = np.block([[wc, -ws], [ws, wc]])
    out[T_W2I] = np.block([[wc.T, ws.T], [-ws.T, wc.T]])
    for m in range(3):
        sc, ss = np.zeros((128, 128)), np.zeros((128, 128))
        for j in range(2):
            rows = slice(48 * j + 16 * m, 48 * j + 16 * m + 16)
            cols = slice(16 * j, 16 * j + 16)
            sc[rows, cols], ss[rows, cols] = cos, sin
        out[T_S2 + m] = np.block([[sc, -ss], [ss, sc]])
        out[T_S2I + m] = np.block([[sc.T, ss.T], [-ss.T, sc.T]])
    return out


def two_parts(value):
    high = value.astype(np.float32).astype(ml_dtypes.bfloat16)
    low = (value - high.astype(np.float64)).astype(np.float32).astype(ml_dtypes.bfloat16)
    return np.stack([high, low])


def twiddles():
    th = 2.0 * math.pi * (np.arange(256)[:, None] * (np.arange(128) % 16)[None, :]) / 4096.0
    ty = angle(16, 128, 4096)
    return np.concatenate([np.cos(th), np.sin(th), np.cos(ty), np.sin(ty)], 0).astype(np.float32)


def split(value):
    high = value.astype(BF16)
    return high, (value - high.astype(F32)).astype(BF16)


def product(a, b, form=(((1,), (0,)), ((), ()))):
    dot = functools.partial(lax.dot_general, dimension_numbers=form, preferred_element_type=F32)
    return dot(a[0], b[0]) + (dot(a[0], b[1]) + dot(a[1], b[0]))


LANES = (((1,), (1,)), ((), ()))


def cross(left, right):
    return [
        left[1] * right[2] - left[2] * right[1],
        left[2] * right[0] - left[0] * right[2],
        left[0] * right[1] - left[1] * right[0],
    ]


def squared(v):
    return v[0] * v[0] + v[1] * v[1] + v[2] * v[2]


def kernel(n_tx, n_ty, mag_h, occ_h, ks_h, cb_h, tw_h, next_ref, rate_ref, mag, occ, ks, cb, tw, m0l, fb, k1, dm, ex,
           mr, mrl, hb, kt, kr, kr2, kst, s1, r1, s2, r2, u, uq, oq, zb, xs, ys, pb, os, load_sem, ty_send, ty_recv,
           h_send, h_recv, k_send, k_recv, a_send, a_recv, b_send, b_recv, f_send, f_recv):
    n = n_tx * n_ty
    tx, ty = lax.axis_index("tx"), lax.axis_index("ty")
    me = tx * n_ty + ty

    loads = [
        pltpu.make_async_copy(mag_h, mag, load_sem.at[0]),
        pltpu.make_async_copy(occ_h, occ, load_sem.at[1]),
        pltpu.make_async_copy(ks_h.at[:, pl.ds(0, 24), :], ks, load_sem.at[2]),
        pltpu.make_async_copy(cb_h, cb, load_sem.at[3]),
        pltpu.make_async_copy(tw_h, tw, load_sem.at[4]),
    ]
    for load in loads:
        load.start()

    barrier = pltpu.get_barrier_semaphore()

    def greet(p, _):
        to = lax.rem(me + p, n)
        pl.semaphore_signal(barrier, inc=1, device_id=(to // n_ty, lax.rem(to, n_ty)), device_id_type=MESH)
        return 0

    lax.fori_loop(1, n, greet, 0)
    loads[0].wait()
    loads[1].wait()
    occf = occ[...].astype(F32)
    for m in range(3):
        m0l[m] = mag[m] * occf
    pl.semaphore_wait(barrier, n - 1)

    def table(k):
        return cb[0, k], cb[1, k]

    mine = pl.ds(pl.multiple_of(ty * 256, 256), 256)

    def ty_out(p, _):
        to = lax.rem(ty + p, n_ty)
        pltpu.make_async_remote_copy(
            src_ref=m0l.at[:, pl.ds(pl.multiple_of(to * 16, 16), 16), :], dst_ref=fb.at[0, :, :, mine],
            send_sem=ty_send, recv_sem=ty_recv, device_id=(tx, to), device_id_type=MESH,
        ).start()
        return 0

    lax.fori_loop(1, n_ty, ty_out, 0)
    own_rows = pl.ds(pl.multiple_of(ty * 16, 16), 16)
    pltpu.make_async_copy(m0l.at[:, own_rows, :], fb.at[0, :, :, mine], ty_recv).start()

    loads[2].wait()
    upper = me >= n // 2
    top = lax.broadcasted_iota(jnp.int32, (8, 256), 0) == 0
    for k in range(4):
        for h in range(2):
            tiles = []
            for d in range(16):
                tile = ks[k, pl.ds(8 * h, 8), pl.ds(256 * d, 256)]
                if h == 0:
                    kr[k, pl.ds(d, 1), :] = ks[k, pl.ds(0, 1), pl.ds(256 * d, 256)]
                    other = ks[k, pl.ds(16, 8), pl.ds(256 * d, 256)]
                    tile = jnp.where(jnp.logical_and(top, upper), other, tile)
                tiles.append(tile)
            kt[k, h] = jnp.concatenate(tiles, 0).T

    def row_copy():
        return pltpu.make_async_remote_copy(
            src_ref=kr, dst_ref=kr2, send_sem=k_send, recv_sem=k_recv, device_id=(0, 0), device_id_type=MESH
        )

    @pl.when(me == n // 2)
    def _():
        row_copy().start()
        row_copy().wait_send()

    loads[3].wait()
    loads[4].wait()
    uq[...] = jnp.zeros_like(uq)

    @pl.when(me == 0)
    def _():
        row_copy().wait_recv()
        for k in range(4):
            rows = jnp.concatenate([kr[k], kr2[k], jnp.zeros((96, 256), F32)], 0)
            kst[k] = rows.T

    pltpu.make_async_copy(fb.at[0], fb.at[0], ty_recv).wait()
    rest = m0l.at[:, pl.ds(0, 16 * (n_ty - 1)), :]
    pltpu.make_async_copy(rest, rest, ty_send).wait()

    def exchange(source, target, send, recv):
        own = pl.ds(pl.multiple_of(me * 4, 4), 4)

        def out(p, _):
            to = lax.rem(me + p, n)
            pltpu.make_async_remote_copy(
                src_ref=source.at[:, pl.ds(pl.multiple_of(to * 4, 4), 4), :], dst_ref=target.at[:, own, :],
                send_sem=send, recv_sem=recv, device_id=(to // n_ty, lax.rem(to, n_ty)), device_id_type=MESH,
            ).start()
            return 0

        lax.fori_loop(1, n, out, 0)
        pltpu.make_async_copy(source.at[:, own, :], target.at[:, own, :], recv).start()

    def arrived(target, recv):
        pltpu.make_async_copy(target, target, recv).wait()

    def sent(source, send):
        rest = source.at[:, pl.ds(0, 4 * (n - 1)), :]
        pltpu.make_async_copy(rest, rest, send).wait()

    lane = lax.broadcasted_iota(jnp.int32, (128, 128), 1)
    after, before = lax.rem(me + 1, n), lax.rem(me + n - 1, n)

    def step(it, _):
        halos = []
        for side, (to, row) in enumerate(((after, 15), (before, 0))):
            halos.append(pltpu.make_async_remote_copy(
                src_ref=fb.at[it, :, row], dst_ref=hb.at[it, side, pl.ds(0, 3)],
                send_sem=h_send.at[side], recv_sem=h_recv.at[it, side],
                device_id=(to // n_ty, lax.rem(to, n_ty)), device_id_type=MESH,
            ))
        for halo in halos:
            halo.start()

        def y_first(m, _):
            a = [fb[it, m, :, pl.ds(128 * k, 128)] for k in range(16)]
            real, imag = [None] * 17, [None] * 17
            for c in range(9):
                sums = []
                for odd in range(2):
                    re, im = None, None
                    for k in range(odd, 16, 2):
                        w = 2.0 * math.pi * (c * k % 32) / 32.0
                        wr, wi = round(math.cos(w), 15), round(-math.sin(w), 15)
                        if wr != 0.0:
                            re = a[k] * wr if re is None else re + a[k] * wr
                        if wi != 0.0:
                            im = a[k] * wi if im is None else im + a[k] * wi
                    zero = jnp.zeros_like(a[0])
                    sums.append((zero if re is None else re, zero if im is None else im))
                (er, ei), (ro, io) = sums
                real[c], imag[c] = er + ro, ei + io
                real[16 - c], imag[16 - c] = er - ro, io - ei
            base = pl.multiple_of(m * 256, 256)
            for c in range(16):
                if c == 0:
                    vr, vi = real[0], real[16]
                else:
                    cos, sin = tw[pl.ds(512 + c, 1), :], tw[pl.ds(528 + c, 1), :]
                    vr, vi = real[c] * cos + imag[c] * sin, imag[c] * cos - real[c] * sin
                for part, v in enumerate((vr, vi)):
                    cols = pl.ds(128 * part, 128)
                    for k, piece in enumerate(split(v)):
                        u[k, pl.ds(base + 16 * c, 16), cols] = piece
                        if c == 0:
                            uq[k, pl.ds(pl.multiple_of(m * 16, 16), 16), cols] = piece
            return 0

        lax.fori_loop(0, 3, y_first, 0)
        oq[...] = product(table(T_WAQ), (uq[0], uq[1]), LANES)

        @pl.when(it == 1)
        def _():
            sent(s1, a_send)

        def y_second(m, _):
            rows = pl.ds(pl.multiple_of(m * 256, 256), 256)
            full = product(table(T_WA), (u[0, rows], u[1, rows]), LANES)
            for part in range(2):
                block = full[128 * part:128 * part + 128]
                own = pltpu.roll(oq[pl.ds(128 * part, 128), :], lax.rem(128 - 16 * m, 128), 1)
                s1[m, pl.ds(2 * part, 128, stride=4), :] = jnp.where(lane < 16, own, block[:, :128])
                s1[m, pl.ds(2 * part + 1, 128, stride=4), :] = block[:, 128:]
            return 0

        lax.fori_loop(0, 3, y_second, 0)
        exchange(s1, r1, a_send, a_recv)

        for halo in halos:
            halo.wait_recv()
        row = lax.broadcasted_iota(jnp.int32, (16, 2048), 0)
        col = lax.broadcasted_iota(jnp.int32, (16, 2048), 1)
        for m in range(3):
            f = fb[it, m]
            low = jnp.where(me > 0, hb[it, 0, pl.ds(m, 1), :], 0.0)
            high = jnp.where(me < n - 1, hb[it, 1, pl.ds(m, 1), :], 0.0)
            up = jnp.where(row == 0, low, pltpu.roll(f, 1, 0))
            down = jnp.where(row == 15, high, pltpu.roll(f, 15, 0))
            left = jnp.where(col == 0, 0.0, pltpu.roll(f, 1, 1))
            right = jnp.where(col == 2047, 0.0, pltpu.roll(f, 2047, 1))
            ex[m] = STIFFNESS * (down + up + right + left)
        for halo in halos:
            halo.wait_send()

        arrived(r1, a_recv)

        def x_forward(m, _):
            for part in range(2):
                for h in range(2):
                    block = r1[m, pl.ds(2 * part + h, 128, stride=4), :]
                    for k, piece in enumerate(split(block)):
                        xs[k, pl.ds(128 * part, 128), pl.ds(128 * h, 128)] = piece
            x = (xs[0], xs[1])
            tr, ti = product(table(T_W1R), x), product(table(T_W1I), x)
            cos, sin = tw[pl.ds(0, 256), :], tw[pl.ds(256, 256), :]
            for h in range(2):
                ar, ai = tr[:, 128 * h:128 * h + 128], ti[:, 128 * h:128 * h + 128]
                v = jnp.concatenate([ar * cos + ai * sin, ai * cos - ar * sin], 1)
                z = product(split(v), table(T_W2))
                zb[m, h, 0] = z[:, :128]
                zb[m, h, 1] = z[:, 128:]
            return 0

        lax.fori_loop(0, 3, x_forward, 0)

        @pl.when(me == 0)
        def _():
            cos, sin = tw[pl.ds(0, 256), :], tw[pl.ds(256, 256), :]
            seq = jnp.zeros((128, 128), F32)
            for j in range(2):
                for m in range(3):
                    block = r1[m, pl.ds(2 * j, 128, stride=4), :]
                    place = 48 * j + 16 * m
                    inside = jnp.logical_and(lane >= place, lane < place + 16)
                    seq = jnp.where(inside, pltpu.roll(block, place, 1) if place else block, seq)
            seq = split(seq)
            ar = product((cb[0, T_W1R][:, :128], cb[1, T_W1R][:, :128]), seq)
            ai = product((cb[0, T_W1I][:, :128], cb[1, T_W1I][:, :128]), seq)
            v = split(jnp.concatenate([ar * cos + ai * sin, ai * cos - ar * sin], 1))
            z = [product(v, table(T_S2 + m)) for m in range(3)]
            two = lambda k: jnp.concatenate([kst[k], kst[k]], 1)
            xx, yy, zz, xy = two(0), two(1), two(2), two(3)
            field = [xx * z[0] + xy * z[1], xy * z[0] + yy * z[1], zz * z[2]]
            back = 0.0
            for m in range(3):
                back = back + product(split(field[m]), table(T_S2I + m))
            br, bi = back[:, :128], back[:, 128:]
            yr, yi = split(br * cos - bi * sin), split(bi * cos + br * sin)
            os[...] = product((cb[0, T_BR][:128], cb[1, T_BR][:128]), yr) + product(
                (cb[0, T_BI][:128], cb[1, T_BI][:128]), yi)

        def gains(k, _):
            h, part = k // 2, lax.rem(k, 2)
            x, y, z = zb[0, h, part], zb[1, h, part], zb[2, h, part]
            xy = kt[3, h]
            zb[0, h, part] = kt[0, h] * x + xy * y
            zb[1, h, part] = xy * x + kt[1, h] * y
            zb[2, h, part] = kt[2, h] * z
            return 0

        lax.fori_loop(0, 4, gains, 0)

        @pl.when(it == 1)
        def _():
            sent(s2, b_send)

        def x_inverse(m, _):
            cos, sin = tw[pl.ds(0, 256), :], tw[pl.ds(256, 256), :]
            for h in range(2):
                field = split(jnp.concatenate([zb[m, h, 0], zb[m, h, 1]], 1))
                p = product(field, table(T_W2I))
                pr, pi = p[:, :128], p[:, 128:]
                for part, v in enumerate((pr * cos - pi * sin, pi * cos + pr * sin)):
                    for k, piece in enumerate(split(v)):
                        ys[k, part, :, pl.ds(128 * h, 128)] = piece
            o = product(table(T_BR), (ys[0, 0], ys[1, 0])) + product(table(T_BI), (ys[0, 1], ys[1, 1]))
            for part in range(2):
                for h in range(2):
                    s2[m, pl.ds(2 * part + h, 128, stride=4), :] = (
                        o[128 * part:128 * part + 128, 128 * h:128 * h + 128])

            @pl.when(me == 0)
            def _():
                for j in range(2):
                    place = pl.ds(2 * j, 128, stride=4)
                    own = pltpu.roll(os[...], 128 - 48 * j - 16 * m, 1)
                    s2[m, place, :] = jnp.where(lane < 16, own, s2[m, place, :])

            return 0

        lax.fori_loop(0, 3, x_inverse, 0)
        exchange(s2, r2, b_send, b_recv)
        arrived(r2, b_recv)

        def y_inverse(m, _):
            for part in range(2):
                for h in range(2):
                    block = r2[m, pl.ds(2 * part + h, 128, stride=4), :].T
                    for k, piece in enumerate(split(block)):
                        xs[k, pl.ds(128 * h, 128), pl.ds(128 * part, 128)] = piece
            pb[...] = product((xs[0], xs[1]), table(T_W3))
            pq = product((xs[0, pl.ds(0, 16), :], xs[1, pl.ds(0, 16), :]), table(T_W3Q))
            real, imag = [None] * 16, [None] * 16
            for c in range(1, 16):
                cos, sin = tw[pl.ds(512 + c, 1), :], tw[pl.ds(528 + c, 1), :]
                br, bi = pb[pl.ds(16 * c, 16), pl.ds(0, 128)], pb[pl.ds(16 * c, 16), pl.ds(128, 128)]
                real[c], imag[c] = br * cos - bi * sin, bi * cos + br * sin
            ends = (pq[:, :128] + pq[:, 128:], pq[:, :128] - pq[:, 128:])
            pairs = []
            for odd in range(2):
                pairs.append([
                    (real[c] - real[16 - c], imag[c] + imag[16 - c]) if odd
                    else (real[c] + real[16 - c], imag[c] - imag[16 - c]) for c in range(1, 8)
                ])
            for a in range(16):
                total = ends[a % 2]
                for c in range(1, 9):
                    re, im = pairs[a % 2][c - 1] if c < 8 else (real[8], imag[8])
                    w = 2.0 * math.pi * (c * a % 32) / 32.0
                    wr, wi = round(math.cos(w), 15), round(math.sin(w), 15)
                    if wr != 0.0:
                        total = total + re * wr
                    if wi != 0.0:
                        total = total - im * wi
                dm[m, :, pl.ds(128 * a, 128)] = total
            return 0

        lax.fori_loop(0, 3, y_inverse, 0)

        def advance(j, _):
            cols = pl.ds(pl.multiple_of(j * 256, 256), 256)
            m0 = [fb[0, m, :, cols] for m in range(3)]
            f = [fb[it, m, :, cols] for m in range(3)]
            heff = [dm[m, :, cols] + ex[m, :, cols] for m in range(3)]
            torque = cross(f, heff)
            damped = cross(f, torque)
            rate = [(t + DAMPING * d) * (-1.0 / (1.0 + DAMPING * DAMPING)) for t, d in zip(torque, damped)]

            @pl.when(it == 0)
            def _():
                filled = jnp.where(squared(m0) > 0.5, 0.0, 1.0)
                v = [m + TIME_STEP * r for m, r in zip(m0, rate)]
                root = jnp.sqrt(squared(v) + filled)
                for m in range(3):
                    k1[m, :, cols] = rate[m]
                    fb[1, m, :, cols] = v[m] / root

            @pl.when(it == 1)
            def _():
                along = rate[0] * m0[0] + rate[1] * m0[1] + rate[2] * m0[2]
                for m in range(3):
                    mr[m, :, cols] = 0.5 * (k1[m, :, cols] + (rate[m] - along * m0[m]))

            return 0

        lax.fori_loop(0, 8, advance, 0)
        return 0

    lax.fori_loop(0, 2, step, 0)
    sent(s1, a_send)
    sent(s2, b_send)

    def back(p, _):
        to = lax.rem(ty + p, n_ty)
        pltpu.make_async_remote_copy(
            src_ref=mr.at[:, :, pl.ds(pl.multiple_of(to * 256, 256), 256)], dst_ref=mrl.at[:, own_rows, :],
            send_sem=f_send, recv_sem=f_recv, device_id=(tx, to), device_id_type=MESH,
        ).start()
        return 0

    lax.fori_loop(1, n_ty, back, 0)
    pltpu.make_async_copy(mr.at[:, :, mine], mrl.at[:, own_rows, :], f_recv).start()
    pltpu.make_async_copy(mrl, mrl, f_recv).wait()
    pltpu.make_async_copy(rest, rest, f_send).wait()

    def finish(j, _):
        rows = pl.ds(pl.multiple_of(j * 16, 16), 16)
        r = [mrl[m, rows, :] for m in range(3)]
        v = [m0l[m, rows, :] + TIME_STEP * r[m] for m in range(3)]
        root = jnp.sqrt(squared(v) + 1.0 - occ[rows, :].astype(F32))
        for m in range(3):
            rate_ref[m, rows, :] = r[m]
            next_ref[m, rows, :] = v[m] / root
        return 0

    lax.fori_loop(0, 8, finish, 0)


def body(n_tx, n_ty, mag, occupancy, kernel_spectrum):
    cb = jnp.asarray(two_parts(matrices()))
    tw = jnp.asarray(twiddles())
    V = pltpu.VMEM
    D = pltpu.SemaphoreType.DMA
    block = (3, 128, 256)
    band = (3, 16, 2048)
    slots = (3, 512, 128)
    out = jax.ShapeDtypeStruct(block, F32)
    return pl.pallas_call(
        functools.partial(kernel, n_tx, n_ty),
        out_shape=(out, out),
        in_specs=[pl.BlockSpec(memory_space=pl.ANY)] * 5,
        out_specs=(pl.BlockSpec(memory_space=pltpu.VMEM),) * 2,
        scratch_shapes=[
            V(block, F32), V((128, 256), jnp.int32), V((4, 24, 4096), F32), V((2, N_TABLES, 256, 256), BF16),
            V((544, 128), F32),
            V(block, F32), V((2,) + band, F32), V(band, F32), V(band, F32), V(band, F32),
            V(band, F32), V(block, F32), V((2, 2, 8, 2048), F32), V((4, 2, 256, 128), F32),
            V((4, 16, 256), F32), V((4, 16, 256), F32), V((4, 256, 128), F32),
            V(slots, F32), V(slots, F32), V(slots, F32), V(slots, F32),
            V((2, 768, 256), BF16), V((2, 128, 256), BF16), V((256, 128), F32), V((3, 2, 2, 256, 128), F32),
            V((2, 256, 256), BF16), V((2, 2, 256, 256), BF16), V((256, 256), F32), V((128, 128), F32),
            D((5,)), D, D, D((2,)), D((2, 2)), D, D, D, D, D, D, D, D,
        ],
        compiler_params=pltpu.CompilerParams(
            collective_id=0, has_side_effects=True, vmem_limit_bytes=56 * 1024 * 1024
        ),
    )(mag, occupancy, kernel_spectrum, cb, tw)


def solution(mesh):
    return jax.shard_map(
        functools.partial(body, mesh.shape["tx"], mesh.shape["ty"]),
        mesh=mesh,
        in_specs=(P(None, "tx", "ty"), P("tx", "ty"), P(None, ("tx", "ty"), None)),
        out_specs=(P(None, "tx", "ty"), P(None, "tx", "ty")),
        check_vma=False,
    )
```

```python
import functools
import itertools
import math

import jax
import jax.numpy as jnp
import ml_dtypes
import numpy as np
from jax import lax
from jax.experimental import pallas as pl
from jax.experimental.pallas import tpu as pltpu
from jax.sharding import PartitionSpec as P

DAMPING = 0.3
STIFFNESS = 0.25
TIME_STEP = 0.25
MESH = pl.DeviceIdType.MESH
F32 = jnp.float32
BF16 = jnp.bfloat16


(T_WA, T_WAQ, T_W1R, T_W1I, T_W2, T_W2I, T_BR, T_BI, T_W3, T_W3Q, T_S2, T_S2I) = (
    0, 1, 2, 3, 4, 5, 6, 7, 8, 9, 10, 13,
)
N_TABLES = 16


def angle(left, right, length):
    product = np.arange(left)[:, None] * np.arange(right)[None, :] % length
    return 2.0 * math.pi * product / length


def matrices():
    out = np.zeros((N_TABLES, 256, 256))
    th = angle(128, 128, 128)
    cos, sin = np.cos(th), np.sin(th)
    out[T_WA] = np.block([[cos, sin], [-sin, cos]])
    scale = -(2.0**-24)
    out[T_W3] = 2.0 * scale * np.block([[cos, sin], [-sin, cos]])
    ph = th + 2.0 * math.pi * np.arange(128)[None, :] / 256.0
    low, high = np.arange(1, 64), np.arange(64, 128)
    sign = 1.0 - 2.0 * (np.arange(128) % 2)
    q = np.zeros((2, 128, 2, 128))
    q[0, 0, 0], q[1, 0, 0] = 1.0, sign
    q[0, low, 0], q[1, low, 0] = cos[low], -sin[low]
    q[0, high, 1], q[1, high, 1] = np.cos(ph)[high], -np.sin(ph)[high]
    out[T_WAQ] = q.reshape(256, 256)
    weight = np.full((128, 1, 1), 2.0)
    weight[0] = 1.0
    out[T_W3Q] = scale * (q * weight).reshape(256, 256)
    th = angle(256, 128, 256)
    cos, sin = np.cos(th), np.sin(th)
    out[T_W1R] = np.concatenate([cos, sin], 1)
    out[T_W1I] = np.concatenate([-sin, cos], 1)
    out[T_BR] = np.concatenate([cos.T, sin.T], 0)
    out[T_BI] = np.concatenate([-sin.T, cos.T], 0)
    th = angle(16, 16, 16)
    cos, sin = np.cos(th), np.sin(th)
    eight = np.eye(8)
    wc = np.einsum("ab,id->aidb", eight, cos).reshape(128, 128)
    ws = np.einsum("ab,id->aidb", eight, sin).reshape(128, 128)
    out[T_W2] = np.block([[wc, -ws], [ws, wc]])
    out[T_W2I] = np.block([[wc.T, ws.T], [-ws.T, wc.T]])
    for m in range(3):
        sc, ss = np.zeros((128, 128)), np.zeros((128, 128))
        for j in range(2):
            rows = slice(48 * j + 16 * m, 48 * j + 16 * m + 16)
            cols = slice(16 * j, 16 * j + 16)
            sc[rows, cols], ss[rows, cols] = cos, sin
        out[T_S2 + m] = np.block([[sc, -ss], [ss, sc]])
        out[T_S2I + m] = np.block([[sc.T, ss.T], [-ss.T, sc.T]])
    return out


def two_parts(value):
    high = value.astype(np.float32).astype(ml_dtypes.bfloat16)
    low = (value - high.astype(np.float64)).astype(np.float32).astype(ml_dtypes.bfloat16)
    return np.stack([high, low])


def twiddles():
    th = 2.0 * math.pi * (np.arange(256)[:, None] * (np.arange(128) % 16)[None, :]) / 4096.0
    ty = angle(16, 128, 4096)
    return np.concatenate([np.cos(th), np.sin(th), np.cos(ty), np.sin(ty)], 0).astype(np.float32)


def split(value):
    high = value.astype(BF16)
    return high, (value - high.astype(F32)).astype(BF16)


def product(a, b, form=(((1,), (0,)), ((), ()))):
    dot = functools.partial(lax.dot_general, dimension_numbers=form, preferred_element_type=F32)
    return dot(a[0], b[0]) + (dot(a[0], b[1]) + dot(a[1], b[0]))


LANES = (((1,), (1,)), ((), ()))


def cross(left, right):
    return [
        left[1] * right[2] - left[2] * right[1],
        left[2] * right[0] - left[0] * right[2],
        left[0] * right[1] - left[1] * right[0],
    ]


def squared(v):
    return v[0] * v[0] + v[1] * v[1] + v[2] * v[2]


def far_first(n_x, n_y, n_z):
    def far(o):
        return sum(min(d, k - d) for d, k in zip(o, (n_x, n_y, n_z)))

    offsets = [o for o in itertools.product(range(n_x), range(n_y), range(n_z), range(2)) if any(o)]
    mixed = np.random.RandomState(1).permutation(len(offsets))
    return sorted((offsets[k] for k in mixed), key=lambda o: -far(o))


def kernel(sizes, mag_h, occ_h, ks_h, cb_h, tw_h, out_ref, mag, occ, ks, cb, tw, m0l, fb, k1, dm, ex,
           mr, hb, kt, kr, kr2, kst, s1, r1, s2, r2, u, zb, xs, ys, pb, os, load_sem, ty_send, ty_recv,
           h_send, h_recv, k_send, k_recv, a_send, a_recv, b_send, b_recv, f_send, f_recv):
    n_x, n_y, n_z = sizes
    n_ty = 2 * n_z
    n = n_x * n_y * n_ty
    tx, ty = lax.axis_index("tx"), lax.axis_index("ty")
    me = tx * n_ty + ty
    px, py, pz, pc = tx // n_y, lax.rem(tx, n_y), ty // 2, lax.rem(ty, 2)
    at_x = [lax.rem(px + d, n_x) * n_y for d in range(n_x)]
    at_y = [lax.rem(py + d, n_y) for d in range(n_y)]
    at_z = [lax.rem(pz + d, n_z) * 2 for d in range(n_z)]
    at_c = [pc, 1 - pc]
    others = far_first(n_x, n_y, n_z)

    loads = [
        pltpu.make_async_copy(mag_h, mag, load_sem.at[0]),
        pltpu.make_async_copy(occ_h, occ, load_sem.at[1]),
        pltpu.make_async_copy(ks_h.at[:, pl.ds(0, 24), :], ks, load_sem.at[2]),
        pltpu.make_async_copy(cb_h, cb, load_sem.at[3]),
        pltpu.make_async_copy(tw_h, tw, load_sem.at[4]),
    ]
    for k in (0, 1, 4, 3, 2):
        loads[k].start()

    barrier = pltpu.get_barrier_semaphore()
    for dx, dy, dz, dc in others:
        to = (at_x[dx] + at_y[dy], at_z[dz] + at_c[dc])
        pl.semaphore_signal(barrier, inc=1, device_id=to, device_id_type=MESH)
    loads[0].wait()
    loads[1].wait()
    occf = occ[...].astype(F32)
    for m in range(3):
        m0l[m] = mag[m] * occf
    pl.semaphore_wait(barrier, n - 1)

    def table(k):
        return cb[0, k], cb[1, k]

    mine = pl.ds(pl.multiple_of(ty * 256, 256), 256)
    own_rows = pl.ds(pl.multiple_of(ty * 16, 16), 16)
    for m in (2, 0, 1):
        for dx, dy, dz, dc in others:
            if dx == 0 and dy == 0:
                to = at_z[dz] + at_c[dc]
                pltpu.make_async_remote_copy(
                    src_ref=m0l.at[m, pl.ds(pl.multiple_of(to * 16, 16), 16), :], dst_ref=fb.at[0, m, :, mine],
                    send_sem=ty_send, recv_sem=ty_recv.at[m], device_id=(tx, to), device_id_type=MESH,
                ).start()
        pltpu.make_async_copy(m0l.at[m, own_rows, :], fb.at[0, m, :, mine], ty_recv.at[m]).start()

    loads[3].wait()
    loads[4].wait()
    own = pl.ds(pl.multiple_of(me * 4, 4), 4)

    def exchange(m, source, target, send, recv):
        for dx, dy, dz, dc in others:
            a, b = at_x[dx] + at_y[dy], at_z[dz] + at_c[dc]
            there = pl.ds(pl.multiple_of((a * n_ty + b) * 4, 4), 4)
            pltpu.make_async_remote_copy(
                src_ref=source.at[m, there, :], dst_ref=target.at[m, own, :],
                send_sem=send, recv_sem=recv.at[m], device_id=(a, b), device_id_type=MESH,
            ).start()
        pltpu.make_async_copy(source.at[m, own, :], target.at[m, own, :], recv.at[m]).start()

    def arrived(m, target, recv):
        pltpu.make_async_copy(target.at[m], target.at[m], recv.at[m]).wait()

    def sent(source, send):
        rest = source.at[:, pl.ds(0, 4 * (n - 1)), :]
        pltpu.make_async_copy(rest, rest, send).wait()

    lane = lax.broadcasted_iota(jnp.int32, (128, 128), 1)
    after, before = lax.rem(me + 1, n), lax.rem(me + n - 1, n)

    def row_copy():
        return pltpu.make_async_remote_copy(
            src_ref=kr, dst_ref=kr2, send_sem=k_send, recv_sem=k_recv, device_id=(0, 0), device_id_type=MESH
        )

    def kernel_tables():
        loads[2].wait()
        upper = me >= n // 2
        top = lax.broadcasted_iota(jnp.int32, (8, 256), 0) == 0
        for k in range(4):
            for d in range(16):
                kr[k, pl.ds(d, 1), :] = ks[k, pl.ds(0, 1), pl.ds(256 * d, 256)]

        @pl.when(me == n // 2)
        def _():
            row_copy().start()

        for k in range(4):
            for h in range(2):
                tiles = []
                for d in range(16):
                    tile = ks[k, pl.ds(8 * h, 8), pl.ds(256 * d, 256)]
                    if h == 0:
                        other = ks[k, pl.ds(16, 8), pl.ds(256 * d, 256)]
                        tile = jnp.where(jnp.logical_and(top, upper), other, tile)
                    tiles.append(tile)
                kt[k, h] = jnp.concatenate(tiles, 0).T

        @pl.when(me == n // 2)
        def _():
            row_copy().wait_send()

        @pl.when(me == 0)
        def _():
            row_copy().wait_recv()
            for k in range(4):
                rows = jnp.concatenate([kr[k], kr2[k], jnp.zeros((96, 256), F32)], 0)
                kst[k] = rows.T

    def step(it, _):
        def y_forward(t, _):
            m = lax.rem(t + 2, 3)

            @pl.when(it == 0)
            def _():
                arrived(m, fb.at[0], ty_recv)

            a = [fb[it, m, :, pl.ds(128 * k, 128)] for k in range(16)]
            real, imag = [None] * 17, [None] * 17
            for c in range(9):
                sums = []
                for odd in range(2):
                    re, im = None, None
                    for k in range(odd, 16, 2):
                        w = 2.0 * math.pi * (c * k % 32) / 32.0
                        wr, wi = round(math.cos(w), 15), round(-math.sin(w), 15)
                        if wr != 0.0:
                            re = a[k] * wr if re is None else re + a[k] * wr
                        if wi != 0.0:
                            im = a[k] * wi if im is None else im + a[k] * wi
                    zero = jnp.zeros_like(a[0])
                    sums.append((zero if re is None else re, zero if im is None else im))
                (er, ei), (ro, io) = sums
                real[c], imag[c] = er + ro, ei + io
                real[16 - c], imag[16 - c] = er - ro, io - ei
            for c in range(16):
                if c == 0:
                    vr, vi = real[0], real[16]
                else:
                    cos, sin = tw[pl.ds(512 + c, 1), :], tw[pl.ds(528 + c, 1), :]
                    vr, vi = real[c] * cos + imag[c] * sin, imag[c] * cos - real[c] * sin
                for part, v in enumerate((vr, vi)):
                    for k, piece in enumerate(split(v)):
                        u[k, pl.ds(16 * c, 16), pl.ds(128 * part, 128)] = piece
            full = product(table(T_WA), (u[0], u[1]), LANES)
            first = product(table(T_WAQ), (u[0, pl.ds(0, 128)], u[1, pl.ds(0, 128)]), LANES)
            for part in range(2):
                rows = slice(128 * part, 128 * part + 128)
                s1[m, pl.ds(2 * part, 128, stride=4), :] = jnp.where(lane < 16, first[rows], full[rows, :128])
                s1[m, pl.ds(2 * part + 1, 128, stride=4), :] = full[rows, 128:]
            exchange(m, s1, r1, a_send, a_recv)
            return 0

        @pl.when(it == 1)
        def _():
            sent(s1, a_send)
            sent(s2, b_send)

        lax.fori_loop(0, 3, y_forward, 0)

        halos = []
        for side, (to, row) in enumerate(((after, 15), (before, 0))):
            halos.append(pltpu.make_async_remote_copy(
                src_ref=fb.at[it, :, row], dst_ref=hb.at[it, side, pl.ds(0, 3)],
                send_sem=h_send.at[side], recv_sem=h_recv.at[it, side],
                device_id=(to // n_ty, lax.rem(to, n_ty)), device_id_type=MESH,
            ))
        for halo in halos:
            halo.start()

        @pl.when(it == 0)
        def _():
            kernel_tables()

        def x_forward(m, _):
            arrived(m, r1, a_recv)
            for part in range(2):
                for h in range(2):
                    block = r1[m, pl.ds(2 * part + h, 128, stride=4), :]
                    for k, piece in enumerate(split(block)):
                        xs[k, pl.ds(128 * part, 128), pl.ds(128 * h, 128)] = piece
            x = (xs[0], xs[1])
            tr, ti = product(table(T_W1R), x), product(table(T_W1I), x)
            cos, sin = tw[pl.ds(0, 256), :], tw[pl.ds(256, 256), :]
            for h in range(2):
                ar, ai = tr[:, 128 * h:128 * h + 128], ti[:, 128 * h:128 * h + 128]
                v = jnp.concatenate([ar * cos + ai * sin, ai * cos - ar * sin], 1)
                z = product(split(v), table(T_W2))
                if isinstance(m, int):
                    zb[m, h, 0] = kt[m, h] * z[:, :128]
                    zb[m, h, 1] = kt[m, h] * z[:, 128:]
                else:
                    zb[m, h, 0] = z[:, :128]
                    zb[m, h, 1] = z[:, 128:]
            return 0

        def mirrored_rows(group):
            cos, sin = tw[pl.ds(0, 256), :], tw[pl.ds(256, 256), :]
            seq = jnp.zeros((128, 128), F32)
            for j in range(2):
                for m in group:
                    block = r1[m, pl.ds(2 * j, 128, stride=4), :]
                    place = 48 * j + 16 * m
                    inside = jnp.logical_and(lane >= place, lane < place + 16)
                    seq = jnp.where(inside, pltpu.roll(block, place, 1) if place else block, seq)
            seq = split(seq)
            ar = product((cb[0, T_W1R][:, :128], cb[1, T_W1R][:, :128]), seq)
            ai = product((cb[0, T_W1I][:, :128], cb[1, T_W1I][:, :128]), seq)
            v = split(jnp.concatenate([ar * cos + ai * sin, ai * cos - ar * sin], 1))
            z = [product(v, table(T_S2 + m)) for m in group]
            two = lambda k: jnp.concatenate([kst[k], kst[k]], 1)
            if len(group) == 1:
                field = [two(2) * z[0]]
            else:
                xx, yy, xy = two(0), two(1), two(3)
                field = [xx * z[0] + xy * z[1], xy * z[0] + yy * z[1]]
            back = 0.0
            for m, f in zip(group, field):
                back = back + product(split(f), table(T_S2I + m))
            br, bi = back[:, :128], back[:, 128:]
            yr, yi = split(br * cos - bi * sin), split(bi * cos + br * sin)
            os[...] = product((cb[0, T_BR][:128], cb[1, T_BR][:128]), yr) + product(
                (cb[0, T_BI][:128], cb[1, T_BI][:128]), yi)

        def gains(k, _):
            h, part = k // 2, lax.rem(k, 2)
            x, y = zb[0, h, part], zb[1, h, part]
            xy = kt[3, h]
            zb[0, h, part] = kt[0, h] * x + xy * y
            zb[1, h, part] = xy * x + kt[1, h] * y
            return 0

        def x_inverse(m, _):
            cos, sin = tw[pl.ds(0, 256), :], tw[pl.ds(256, 256), :]
            for h in range(2):
                field = split(jnp.concatenate([zb[m, h, 0], zb[m, h, 1]], 1))
                p = product(field, table(T_W2I))
                pr, pi = p[:, :128], p[:, 128:]
                for part, v in enumerate((pr * cos - pi * sin, pi * cos + pr * sin)):
                    for k, piece in enumerate(split(v)):
                        ys[k, part, :, pl.ds(128 * h, 128)] = piece
            o = product(table(T_BR), (ys[0, 0], ys[1, 0])) + product(table(T_BI), (ys[0, 1], ys[1, 1]))
            for part in range(2):
                for h in range(2):
                    s2[m, pl.ds(2 * part + h, 128, stride=4), :] = (
                        o[128 * part:128 * part + 128, 128 * h:128 * h + 128])

            @pl.when(me == 0)
            def _():
                for j in range(2):
                    place = pl.ds(2 * j, 128, stride=4)
                    moved = pltpu.roll(os[...], 128 - 48 * j - 16 * m, 1)
                    s2[m, place, :] = jnp.where(lane < 16, moved, s2[m, place, :])

            exchange(m, s2, r2, b_send, b_recv)
            return 0

        x_forward(2, 0)

        @pl.when(me == 0)
        def _():
            mirrored_rows((2,))

        x_inverse(2, 0)
        lax.fori_loop(0, 2, x_forward, 0)

        @pl.when(me == 0)
        def _():
            mirrored_rows((0, 1))

        lax.fori_loop(0, 4, gains, 0)
        lax.fori_loop(0, 2, x_inverse, 0)

        for halo in halos:
            halo.wait_recv()
        row = lax.broadcasted_iota(jnp.int32, (16, 2048), 0)
        col = lax.broadcasted_iota(jnp.int32, (16, 2048), 1)
        for m in range(3):
            f = fb[it, m]
            low = jnp.where(me > 0, hb[it, 0, pl.ds(m, 1), :], 0.0)
            high = jnp.where(me < n - 1, hb[it, 1, pl.ds(m, 1), :], 0.0)
            up = jnp.where(row == 0, low, pltpu.roll(f, 1, 0))
            down = jnp.where(row == 15, high, pltpu.roll(f, 15, 0))
            left = jnp.where(col == 0, 0.0, pltpu.roll(f, 1, 1))
            right = jnp.where(col == 2047, 0.0, pltpu.roll(f, 2047, 1))
            ex[m] = STIFFNESS * (down + up + right + left)
        for halo in halos:
            halo.wait_send()

        def y_inverse(t, _):
            m = lax.rem(t + 2, 3)
            arrived(m, r2, b_recv)
            for part in range(2):
                for h in range(2):
                    block = r2[m, pl.ds(2 * part + h, 128, stride=4), :].T
                    for k, piece in enumerate(split(block)):
                        xs[k, pl.ds(128 * h, 128), pl.ds(128 * part, 128)] = piece
            pb[...] = product((xs[0], xs[1]), table(T_W3))
            pq = product((xs[0, pl.ds(0, 16), :], xs[1, pl.ds(0, 16), :]), table(T_W3Q))
            real, imag = [None] * 16, [None] * 16
            for c in range(1, 16):
                cos, sin = tw[pl.ds(512 + c, 1), :], tw[pl.ds(528 + c, 1), :]
                br, bi = pb[pl.ds(16 * c, 16), pl.ds(0, 128)], pb[pl.ds(16 * c, 16), pl.ds(128, 128)]
                real[c], imag[c] = br * cos - bi * sin, bi * cos + br * sin
            ends = (pq[:, :128] + pq[:, 128:], pq[:, :128] - pq[:, 128:])
            pairs = []
            for odd in range(2):
                pairs.append([
                    (real[c] - real[16 - c], imag[c] + imag[16 - c]) if odd
                    else (real[c] + real[16 - c], imag[c] - imag[16 - c]) for c in range(1, 8)
                ])
            for a in range(16):
                total = ends[a % 2]
                for c in range(1, 9):
                    re, im = pairs[a % 2][c - 1] if c < 8 else (real[8], imag[8])
                    w = 2.0 * math.pi * (c * a % 32) / 32.0
                    wr, wi = round(math.cos(w), 15), round(math.sin(w), 15)
                    if wr != 0.0:
                        total = total + re * wr
                    if wi != 0.0:
                        total = total - im * wi
                dm[m, :, pl.ds(128 * a, 128)] = total
            return 0

        lax.fori_loop(0, 3, y_inverse, 0)

        def advance(j, _):
            far = j // 2
            dz = jnp.where(far == 0, 2, jnp.where(far == 1, 1, jnp.where(far == 2, 3, 0)))
            to = lax.rem(pz + dz, n_z) * 2 + lax.rem(pc + j + 1, 2)
            cols = pl.ds(pl.multiple_of(to * 256, 256), 256)
            m0 = [fb[0, m, :, cols] for m in range(3)]
            f = [fb[it, m, :, cols] for m in range(3)]
            heff = [dm[m, :, cols] + ex[m, :, cols] for m in range(3)]
            torque = cross(f, heff)
            damped = cross(f, torque)
            rate = [(t + DAMPING * d) * (-1.0 / (1.0 + DAMPING * DAMPING)) for t, d in zip(torque, damped)]

            @pl.when(it == 0)
            def _():
                filled = jnp.where(squared(m0) > 0.5, 0.0, 1.0)
                v = [m + TIME_STEP * r for m, r in zip(m0, rate)]
                root = jnp.sqrt(squared(v) + filled)
                for m in range(3):
                    k1[m, :, cols] = rate[m]
                    fb[1, m, :, cols] = v[m] / root

            @pl.when(it == 1)
            def _():
                along = rate[0] * m0[0] + rate[1] * m0[1] + rate[2] * m0[2]
                for m in range(3):
                    mr[m, :, cols] = k1[m, :, cols] + (rate[m] - along * m0[m])

                @pl.when(j < n_ty - 1)
                def _():
                    pltpu.make_async_remote_copy(
                        src_ref=mr.at[:, :, cols], dst_ref=out_ref.at[:, own_rows, :],
                        send_sem=f_send, recv_sem=f_recv, device_id=(tx, to), device_id_type=MESH,
                    ).start()

                @pl.when(j == n_ty - 1)
                def _():
                    pltpu.make_async_copy(mr.at[:, :, cols], out_ref.at[:, own_rows, :], f_recv).start()

            return 0

        lax.fori_loop(0, n_ty, advance, 0)
        return 0

    lax.fori_loop(0, 2, step, 0)
    rest = m0l.at[:, pl.ds(0, 16 * (n_ty - 1)), :]
    pltpu.make_async_copy(rest, rest, ty_send).wait()
    sent(s1, a_send)
    sent(s2, b_send)
    pltpu.make_async_copy(out_ref, out_ref, f_recv).wait()
    pltpu.make_async_copy(rest, rest, f_send).wait()


def body(sizes, mag, occupancy, kernel_spectrum):
    cb = jnp.asarray(two_parts(matrices()))
    tw = jnp.asarray(twiddles())
    V = pltpu.VMEM
    D = pltpu.SemaphoreType.DMA
    block = (3, 128, 256)
    band = (3, 16, 2048)
    slots = (3, 512, 128)
    doubled = pl.pallas_call(
        functools.partial(kernel, sizes),
        out_shape=jax.ShapeDtypeStruct(block, F32),
        in_specs=[pl.BlockSpec(memory_space=pl.ANY)] * 5,
        out_specs=pl.BlockSpec(memory_space=pltpu.VMEM),
        scratch_shapes=[
            V(block, F32), V((128, 256), jnp.int32), V((4, 24, 4096), F32), V((2, N_TABLES, 256, 256), BF16),
            V((544, 128), F32),
            V(block, F32), V((2,) + band, F32), V(band, F32), V(band, F32), V(band, F32),
            V(band, F32), V((2, 2, 8, 2048), F32), V((4, 2, 256, 128), F32),
            V((4, 16, 256), F32), V((4, 16, 256), F32), V((4, 256, 128), F32),
            V(slots, F32), V(slots, F32), V(slots, F32), V(slots, F32),
            V((2, 256, 256), BF16), V((3, 2, 2, 256, 128), F32),
            V((2, 256, 256), BF16), V((2, 2, 256, 256), BF16), V((256, 256), F32), V((128, 128), F32),
            D((5,)), D, D((3,)), D((2,)), D((2, 2)), D, D, D, D((3,)), D, D((3,)), D, D,
        ],
        compiler_params=pltpu.CompilerParams(
            collective_id=0, has_side_effects=True, vmem_limit_bytes=56 * 1024 * 1024
        ),
    )(mag, occupancy, kernel_spectrum, cb, tw)
    occ = occupancy.astype(F32)
    mean_rate = 0.5 * doubled
    v = mag * occ[None] + TIME_STEP * mean_rate
    root = jnp.sqrt(jnp.sum(v * v, axis=0) + 1.0 - occ)
    return v / root[None], mean_rate


def solution(mesh):
    n_tx, n_ty = mesh.shape["tx"], mesh.shape["ty"]
    side = math.isqrt(n_tx)
    return jax.shard_map(
        functools.partial(body, (side, side, n_ty // 2)),
        mesh=mesh,
        in_specs=(P(None, "tx", "ty"), P("tx", "ty"), P(None, ("tx", "ty"), None)),
        out_specs=(P(None, "tx", "ty"), P(None, "tx", "ty")),
        check_vma=False,
    )
```

```python
import functools
import itertools
import math

import jax
import jax.numpy as jnp
import ml_dtypes
import numpy as np
from jax import lax
from jax.experimental import pallas as pl
from jax.experimental.pallas import tpu as pltpu
from jax.sharding import PartitionSpec as P

DAMPING = 0.3
STIFFNESS = 0.25
TIME_STEP = 0.25
MESH = pl.DeviceIdType.MESH
F32 = jnp.float32
BF16 = jnp.bfloat16


(T_WA, T_WAQ, T_W1R, T_W1I, T_W2, T_W2I, T_BR, T_BI, T_W3, T_W3Q, T_S2, T_S2I) = (
    0, 1, 2, 3, 4, 5, 6, 7, 8, 9, 10, 13,
)
N_TABLES = 16


def angle(left, right, length):
    product = np.arange(left)[:, None] * np.arange(right)[None, :] % length
    return 2.0 * math.pi * product / length


def matrices():
    out = np.zeros((N_TABLES, 256, 256))
    th = angle(128, 128, 128)
    cos, sin = np.cos(th), np.sin(th)
    out[T_WA] = np.block([[cos, sin], [-sin, cos]])
    scale = -(2.0**-24)
    out[T_W3] = 2.0 * scale * np.block([[cos, sin], [-sin, cos]])
    ph = th + 2.0 * math.pi * np.arange(128)[None, :] / 256.0
    low, high = np.arange(1, 64), np.arange(64, 128)
    sign = 1.0 - 2.0 * (np.arange(128) % 2)
    q = np.zeros((2, 128, 2, 128))
    q[0, 0, 0], q[1, 0, 0] = 1.0, sign
    q[0, low, 0], q[1, low, 0] = cos[low], -sin[low]
    q[0, high, 1], q[1, high, 1] = np.cos(ph)[high], -np.sin(ph)[high]
    out[T_WAQ] = q.reshape(256, 256)
    weight = np.full((128, 1, 1), 2.0)
    weight[0] = 1.0
    out[T_W3Q] = scale * (q * weight).reshape(256, 256)
    th = angle(256, 128, 256)
    cos, sin = np.cos(th), np.sin(th)
    out[T_W1R] = np.concatenate([cos, sin], 1)
    out[T_W1I] = np.concatenate([-sin, cos], 1)
    out[T_BR] = np.concatenate([cos.T, sin.T], 0)
    out[T_BI] = np.concatenate([-sin.T, cos.T], 0)
    th = angle(16, 16, 16)
    cos, sin = np.cos(th), np.sin(th)
    eight = np.eye(8)
    wc = np.einsum("ab,id->aidb", eight, cos).reshape(128, 128)
    ws = np.einsum("ab,id->aidb", eight, sin).reshape(128, 128)
    out[T_W2] = np.block([[wc, -ws], [ws, wc]])
    out[T_W2I] = np.block([[wc.T, ws.T], [-ws.T, wc.T]])
    for m in range(3):
        sc, ss = np.zeros((128, 128)), np.zeros((128, 128))
        for j in range(2):
            rows = slice(48 * j + 16 * m, 48 * j + 16 * m + 16)
            cols = slice(16 * j, 16 * j + 16)
            sc[rows, cols], ss[rows, cols] = cos, sin
        out[T_S2 + m] = np.block([[sc, -ss], [ss, sc]])
        out[T_S2I + m] = np.block([[sc.T, ss.T], [-ss.T, sc.T]])
    return out


def two_parts(value):
    high = value.astype(np.float32).astype(ml_dtypes.bfloat16)
    low = (value - high.astype(np.float64)).astype(np.float32).astype(ml_dtypes.bfloat16)
    return np.stack([high, low])


def twiddles():
    th = 2.0 * math.pi * (np.arange(256)[:, None] * (np.arange(128) % 16)[None, :]) / 4096.0
    ty = angle(16, 128, 4096)
    return np.concatenate([np.cos(th), np.sin(th), np.cos(ty), np.sin(ty)], 0).astype(np.float32)


def split(value):
    high = value.astype(BF16)
    return high, (value - high.astype(F32)).astype(BF16)


def product(a, b, form=(((1,), (0,)), ((), ()))):
    dot = functools.partial(lax.dot_general, dimension_numbers=form, preferred_element_type=F32)
    return dot(a[0], b[0]) + (dot(a[0], b[1]) + dot(a[1], b[0]))


LANES = (((1,), (1,)), ((), ()))


def cross(left, right):
    return [
        left[1] * right[2] - left[2] * right[1],
        left[2] * right[0] - left[0] * right[2],
        left[0] * right[1] - left[1] * right[0],
    ]


def squared(v):
    return v[0] * v[0] + v[1] * v[1] + v[2] * v[2]


def far_first(n_x, n_y, n_z):
    def far(o):
        return sum(min(d, k - d) for d, k in zip(o, (n_x, n_y, n_z)))

    offsets = [o for o in itertools.product(range(n_x), range(n_y), range(n_z), range(2)) if any(o)]
    mixed = np.random.RandomState(1).permutation(len(offsets))
    return sorted((offsets[k] for k in mixed), key=lambda o: -far(o))


def kernel(sizes, mag_h, occ_h, ks_h, cb_h, tw_h, out_ref, mag, occ, ks, cb, tw, m0l, fb, k1, dm, ex,
           mr, hb, kt, kr, kr2, kst, s1, r1, s2, r2, u, zb, xs, ys, pb, pq, os, load_sem, ty_send, ty_recv,
           h_send, h_recv, k_send, k_recv, a_send, a_recv, b_send, b_recv, f_send, f_recv, ready):
    n_x, n_y, n_z = sizes
    n_ty = 2 * n_z
    n = n_x * n_y * n_ty
    tx, ty = lax.axis_index("tx"), lax.axis_index("ty")
    me = tx * n_ty + ty
    px, py, pz, pc = tx // n_y, lax.rem(tx, n_y), ty // 2, lax.rem(ty, 2)
    at_x = [lax.rem(px + d, n_x) * n_y for d in range(n_x)]
    at_y = [lax.rem(py + d, n_y) for d in range(n_y)]
    at_z = [lax.rem(pz + d, n_z) * 2 for d in range(n_z)]
    at_c = [pc, 1 - pc]
    others = far_first(n_x, n_y, n_z)

    loads = [
        pltpu.make_async_copy(mag_h, mag, load_sem.at[0]),
        pltpu.make_async_copy(occ_h, occ, load_sem.at[1]),
        pltpu.make_async_copy(ks_h.at[:, pl.ds(0, 24), :], ks, load_sem.at[2]),
        pltpu.make_async_copy(cb_h, cb, load_sem.at[3]),
        pltpu.make_async_copy(tw_h, tw, load_sem.at[4]),
    ]
    for k in (0, 1, 4, 3, 2):
        loads[k].start()

    barrier = pltpu.get_barrier_semaphore()
    line = [o for o in others if o[:2] == (0, 0)]
    plane = [o for o in others if o[2:] == (0, 0)]
    for dx, dy, dz, dc in plane + line:
        to = (at_x[dx] + at_y[dy], at_z[dz] + at_c[dc])
        pl.semaphore_signal(barrier, inc=1, device_id=to, device_id_type=MESH)
    loads[0].wait()
    loads[1].wait()
    occf = occ[...].astype(F32)
    for m in range(3):
        m0l[m] = mag[m] * occf
    pl.semaphore_wait(barrier, len(plane) + len(line))

    def table(k):
        return cb[0, k], cb[1, k]

    mine = pl.ds(pl.multiple_of(ty * 256, 256), 256)
    own_rows = pl.ds(pl.multiple_of(ty * 16, 16), 16)
    for m in (2, 0, 1):
        for _, _, dz, dc in line:
            to = at_z[dz] + at_c[dc]
            pltpu.make_async_remote_copy(
                src_ref=m0l.at[m, pl.ds(pl.multiple_of(to * 16, 16), 16), :], dst_ref=fb.at[0, m, :, mine],
                send_sem=ty_send, recv_sem=ty_recv.at[m], device_id=(tx, to), device_id_type=MESH,
            ).start()
        pltpu.make_async_copy(m0l.at[m, own_rows, :], fb.at[0, m, :, mine], ty_recv.at[m]).start()

    for _, _, dz, dc in line:
        pl.semaphore_signal(ready, inc=1, device_id=(tx, at_z[dz] + at_c[dc]), device_id_type=MESH)
    loads[3].wait()
    loads[4].wait()
    pl.semaphore_wait(ready, len(line))
    own = pl.ds(pl.multiple_of(me * 4, 4), 4)

    def exchange(m, source, target, send, recv):
        for dx, dy, dz, dc in others:
            a, b = at_x[dx] + at_y[dy], at_z[dz] + at_c[dc]
            there = pl.ds(pl.multiple_of((a * n_ty + b) * 4, 4), 4)
            pltpu.make_async_remote_copy(
                src_ref=source.at[m, there, :], dst_ref=target.at[m, own, :],
                send_sem=send, recv_sem=recv.at[m], device_id=(a, b), device_id_type=MESH,
            ).start()
        pltpu.make_async_copy(source.at[m, own, :], target.at[m, own, :], recv.at[m]).start()

    def arrived(m, target, recv):
        pltpu.make_async_copy(target.at[m], target.at[m], recv.at[m]).wait()

    def sent(source, send):
        rest = source.at[:, pl.ds(0, 4 * (n - 1)), :]
        pltpu.make_async_copy(rest, rest, send).wait()

    lane = lax.broadcasted_iota(jnp.int32, (128, 128), 1)
    after, before = lax.rem(me + 1, n), lax.rem(me + n - 1, n)

    def row_copy():
        return pltpu.make_async_remote_copy(
            src_ref=kr, dst_ref=kr2, send_sem=k_send, recv_sem=k_recv, device_id=(0, 0), device_id_type=MESH
        )

    def kernel_tables():
        loads[2].wait()
        upper = me >= n // 2
        top = lax.broadcasted_iota(jnp.int32, (8, 256), 0) == 0
        for k in range(4):
            for d in range(16):
                kr[k, pl.ds(d, 1), :] = ks[k, pl.ds(0, 1), pl.ds(256 * d, 256)]

        @pl.when(me == n // 2)
        def _():
            row_copy().start()

        for k in range(4):
            for h in range(2):
                tiles = []
                for d in range(16):
                    tile = ks[k, pl.ds(8 * h, 8), pl.ds(256 * d, 256)]
                    if h == 0:
                        other = ks[k, pl.ds(16, 8), pl.ds(256 * d, 256)]
                        tile = jnp.where(jnp.logical_and(top, upper), other, tile)
                    tiles.append(tile)
                kt[k, h] = jnp.concatenate(tiles, 0).T

        @pl.when(me == n // 2)
        def _():
            row_copy().wait_send()

        @pl.when(me == 0)
        def _():
            row_copy().wait_recv()
            for k in range(4):
                rows = jnp.concatenate([kr[k], kr2[k], jnp.zeros((96, 256), F32)], 0)
                kst[k] = rows.T

    def step(it, _):
        def place(m, c):
            if isinstance(m, int) and m == 2:
                return 0, 16 * c
            return 1 + c // 8, pl.multiple_of(128 * m + 16 * (c % 8), 16)

        def y_first(m, _):
            @pl.when(it == 0)
            def _():
                arrived(m, fb.at[0], ty_recv)

            a = [fb[it, m, :, pl.ds(128 * k, 128)] for k in range(16)]
            real, imag = [None] * 17, [None] * 17
            for c in range(9):
                sums = []
                for odd in range(2):
                    re, im = None, None
                    for k in range(odd, 16, 2):
                        w = 2.0 * math.pi * (c * k % 32) / 32.0
                        wr, wi = round(math.cos(w), 15), round(-math.sin(w), 15)
                        if wr != 0.0:
                            re = a[k] * wr if re is None else re + a[k] * wr
                        if wi != 0.0:
                            im = a[k] * wi if im is None else im + a[k] * wi
                    zero = jnp.zeros_like(a[0])
                    sums.append((zero if re is None else re, zero if im is None else im))
                (er, ei), (ro, io) = sums
                real[c], imag[c] = er + ro, ei + io
                real[16 - c], imag[16 - c] = er - ro, io - ei
            for c in range(16):
                if c == 0:
                    vr, vi = real[0], real[16]
                else:
                    cos, sin = tw[pl.ds(512 + c, 1), :], tw[pl.ds(528 + c, 1), :]
                    vr, vi = real[c] * cos + imag[c] * sin, imag[c] * cos - real[c] * sin
                chunk, start = place(m, c)
                for part, v in enumerate((vr, vi)):
                    for k, piece in enumerate(split(v)):
                        u[k, chunk, pl.ds(start, 16), pl.ds(128 * part, 128)] = piece
            return 0

        def y_second(g, _):
            full = product(table(T_WA), (u[0, g], u[1, g]), LANES)
            first = product(table(T_WAQ), (u[0, g], u[1, g]), LANES)
            for part in range(2):
                for b in range(2):
                    block = (slice(128 * part, 128 * part + 128), slice(128 * b, 128 * b + 128))
                    inside = jnp.logical_and(lane < 16, g == 1 if b else g < 2)
                    s1[g, pl.ds(2 * part + b, 128, stride=4), :] = jnp.where(inside, first[block], full[block])
            exchange(g, s1, r1, a_send, a_recv)
            return 0

        @pl.when(it == 1)
        def _():
            sent(s1, a_send)
            sent(s2, b_send)

        y_first(2, 0)
        y_second(0, 0)
        lax.fori_loop(0, 2, y_first, 0)
        lax.fori_loop(1, 3, y_second, 0)

        halos = []
        for side, (to, row) in enumerate(((after, 15), (before, 0))):
            halos.append(pltpu.make_async_remote_copy(
                src_ref=fb.at[it, :, row], dst_ref=hb.at[it, side, pl.ds(0, 3)],
                send_sem=h_send.at[side], recv_sem=h_recv.at[it, side],
                device_id=(to // n_ty, lax.rem(to, n_ty)), device_id_type=MESH,
            ))
        for halo in halos:
            halo.start()

        @pl.when(it == 0)
        def _():
            kernel_tables()

        def mirrored_rows(g, group):
            cos, sin = tw[pl.ds(0, 256), :], tw[pl.ds(256, 256), :]
            seq = jnp.zeros((128, 128), F32)
            for j in range(2):
                for b, m in enumerate(group):
                    block = r1[g, pl.ds(2 * j + b, 128, stride=4), :]
                    at = 48 * j + 16 * m
                    inside = jnp.logical_and(lane >= at, lane < at + 16)
                    seq = jnp.where(inside, pltpu.roll(block, at, 1) if at else block, seq)
            seq = split(seq)
            ar = product((cb[0, T_W1R][:, :128], cb[1, T_W1R][:, :128]), seq)
            ai = product((cb[0, T_W1I][:, :128], cb[1, T_W1I][:, :128]), seq)
            v = split(jnp.concatenate([ar * cos + ai * sin, ai * cos - ar * sin], 1))
            z = [product(v, table(T_S2 + m)) for m in group]
            two = lambda k: jnp.concatenate([kst[k], kst[k]], 1)
            if len(group) == 1:
                field = [two(2) * z[0]]
            else:
                xx, yy, xy = two(0), two(1), two(3)
                field = [xx * z[0] + xy * z[1], xy * z[0] + yy * z[1]]
            back = 0.0
            for m, f in zip(group, field):
                back = back + product(split(f), table(T_S2I + m))
            br, bi = back[:, :128], back[:, 128:]
            yr, yi = split(br * cos - bi * sin), split(bi * cos + br * sin)
            os[...] = product((cb[0, T_BR][:128], cb[1, T_BR][:128]), yr) + product(
                (cb[0, T_BI][:128], cb[1, T_BI][:128]), yi)

        def x_chunk(g, group):
            arrived(g, r1, a_recv)
            for part in range(2):
                for b in range(2):
                    block = r1[g, pl.ds(2 * part + b, 128, stride=4), :]
                    for k, piece in enumerate(split(block)):
                        xs[k, pl.ds(128 * part, 128), pl.ds(128 * b, 128)] = piece
            x = (xs[0], xs[1])
            tr, ti = product(table(T_W1R), x), product(table(T_W1I), x)
            cos, sin = tw[pl.ds(0, 256), :], tw[pl.ds(256, 256), :]
            for b in range(2):
                ar, ai = tr[:, 128 * b:128 * b + 128], ti[:, 128 * b:128 * b + 128]
                v = jnp.concatenate([ar * cos + ai * sin, ai * cos - ar * sin], 1)
                zb[b] = product(split(v), table(T_W2))

            mirrored = me == 0 if len(group) == 1 else jnp.logical_and(me == 0, g == 1)

            @pl.when(mirrored)
            def _():
                mirrored_rows(g, group)

            for b in range(2):
                pieces = []
                for part in range(2):
                    cols = pl.ds(128 * part, 128)
                    if len(group) == 1:
                        pieces.append(kt[2, b] * zb[b, :, cols])
                    else:
                        pieces.append(kt[b, g - 1] * zb[b, :, cols] + kt[3, g - 1] * zb[1 - b, :, cols])
                p = product(split(jnp.concatenate(pieces, 1)), table(T_W2I))
                pr, pi = p[:, :128], p[:, 128:]
                for part, v in enumerate((pr * cos - pi * sin, pi * cos + pr * sin)):
                    for k, piece in enumerate(split(v)):
                        ys[k, part, :, pl.ds(128 * b, 128)] = piece
            o = product(table(T_BR), (ys[0, 0], ys[1, 0])) + product(table(T_BI), (ys[0, 1], ys[1, 1]))
            for part in range(2):
                for b in range(2):
                    s2[g, pl.ds(2 * part + b, 128, stride=4), :] = (
                        o[128 * part:128 * part + 128, 128 * b:128 * b + 128])

            @pl.when(mirrored)
            def _():
                for j in range(2):
                    for b, m in enumerate(group):
                        rows = pl.ds(2 * j + b, 128, stride=4)
                        shift = (128 - 48 * j - 16 * m) % 128
                        moved = pltpu.roll(os[...], shift, 1) if shift else os[...]
                        s2[g, rows, :] = jnp.where(lane < 16, moved, s2[g, rows, :])

            exchange(g, s2, r2, b_send, b_recv)

        def xy_chunk(g, _):
            x_chunk(g, (0, 1))
            return 0

        x_chunk(0, (2,))
        lax.fori_loop(1, 3, xy_chunk, 0)

        for halo in halos:
            halo.wait_recv()
        row = lax.broadcasted_iota(jnp.int32, (16, 2048), 0)
        col = lax.broadcasted_iota(jnp.int32, (16, 2048), 1)
        for m in range(3):
            f = fb[it, m]
            low = jnp.where(me > 0, hb[it, 0, pl.ds(m, 1), :], 0.0)
            high = jnp.where(me < n - 1, hb[it, 1, pl.ds(m, 1), :], 0.0)
            up = jnp.where(row == 0, low, pltpu.roll(f, 1, 0))
            down = jnp.where(row == 15, high, pltpu.roll(f, 15, 0))
            left = jnp.where(col == 0, 0.0, pltpu.roll(f, 1, 1))
            right = jnp.where(col == 2047, 0.0, pltpu.roll(f, 2047, 1))
            ex[m] = STIFFNESS * (down + up + right + left)
        for halo in halos:
            halo.wait_send()

        def y_inverse_first(g, _):
            arrived(g, r2, b_recv)
            for part in range(2):
                for b in range(2):
                    block = r2[g, pl.ds(2 * part + b, 128, stride=4), :].T
                    for k, piece in enumerate(split(block)):
                        xs[k, pl.ds(128 * b, 128), pl.ds(128 * part, 128)] = piece
            pb[g] = product((xs[0], xs[1]), table(T_W3))

            def ends(m, row):
                rows = pl.ds(row, 16)
                pq[m] = product((xs[0, rows, :], xs[1, rows, :]), table(T_W3Q))

            if isinstance(g, int):
                ends(2, 0)
            else:
                @pl.when(g == 1)
                def _():
                    ends(0, 0)
                    ends(1, 128)

            return 0

        def y_inverse_second(m, _):
            real, imag = [None] * 16, [None] * 16
            for c in range(1, 16):
                cos, sin = tw[pl.ds(512 + c, 1), :], tw[pl.ds(528 + c, 1), :]
                chunk, start = place(m, c)
                br, bi = pb[chunk, pl.ds(start, 16), pl.ds(0, 128)], pb[chunk, pl.ds(start, 16), pl.ds(128, 128)]
                real[c], imag[c] = br * cos - bi * sin, bi * cos + br * sin
            even, odd_part = pq[m, :, pl.ds(0, 128)], pq[m, :, pl.ds(128, 128)]
            ends = (even + odd_part, even - odd_part)
            pairs = []
            for odd in range(2):
                pairs.append([
                    (real[c] - real[16 - c], imag[c] + imag[16 - c]) if odd
                    else (real[c] + real[16 - c], imag[c] - imag[16 - c]) for c in range(1, 8)
                ])
            for a in range(16):
                total = ends[a % 2]
                for c in range(1, 9):
                    re, im = pairs[a % 2][c - 1] if c < 8 else (real[8], imag[8])
                    w = 2.0 * math.pi * (c * a % 32) / 32.0
                    wr, wi = round(math.cos(w), 15), round(math.sin(w), 15)
                    if wr != 0.0:
                        total = total + re * wr
                    if wi != 0.0:
                        total = total - im * wi
                dm[m, :, pl.ds(128 * a, 128)] = total
            return 0

        y_inverse_first(0, 0)
        y_inverse_second(2, 0)
        lax.fori_loop(1, 3, y_inverse_first, 0)
        lax.fori_loop(0, 2, y_inverse_second, 0)

        def advance(j, _):
            far = j // 2
            dz = jnp.where(far == 0, 2, jnp.where(far == 1, 1, jnp.where(far == 2, 3, 0)))
            to = lax.rem(pz + dz, n_z) * 2 + lax.rem(pc + j + 1, 2)
            cols = pl.ds(pl.multiple_of(to * 256, 256), 256)
            m0 = [fb[0, m, :, cols] for m in range(3)]
            f = [fb[it, m, :, cols] for m in range(3)]
            heff = [dm[m, :, cols] + ex[m, :, cols] for m in range(3)]
            torque = cross(f, heff)
            damped = cross(f, torque)
            rate = [(t + DAMPING * d) * (-1.0 / (1.0 + DAMPING * DAMPING)) for t, d in zip(torque, damped)]

            @pl.when(it == 0)
            def _():
                filled = jnp.where(squared(m0) > 0.5, 0.0, 1.0)
                v = [m + TIME_STEP * r for m, r in zip(m0, rate)]
                root = jnp.sqrt(squared(v) + filled)
                for m in range(3):
                    k1[m, :, cols] = rate[m]
                    fb[1, m, :, cols] = v[m] / root

            @pl.when(it == 1)
            def _():
                along = rate[0] * m0[0] + rate[1] * m0[1] + rate[2] * m0[2]
                for m in range(3):
                    mr[m, :, cols] = k1[m, :, cols] + (rate[m] - along * m0[m])

                @pl.when(j < n_ty - 1)
                def _():
                    pltpu.make_async_remote_copy(
                        src_ref=mr.at[:, :, cols], dst_ref=out_ref.at[:, own_rows, :],
                        send_sem=f_send, recv_sem=f_recv, device_id=(tx, to), device_id_type=MESH,
                    ).start()

                @pl.when(j == n_ty - 1)
                def _():
                    pltpu.make_async_copy(mr.at[:, :, cols], out_ref.at[:, own_rows, :], f_recv).start()

            return 0

        lax.fori_loop(0, n_ty, advance, 0)
        return 0

    lax.fori_loop(0, 2, step, 0)
    rest = m0l.at[:, pl.ds(0, 16 * (n_ty - 1)), :]
    pltpu.make_async_copy(rest, rest, ty_send).wait()
    sent(s1, a_send)
    sent(s2, b_send)
    pltpu.make_async_copy(out_ref, out_ref, f_recv).wait()
    pltpu.make_async_copy(rest, rest, f_send).wait()


def body(sizes, mag, occupancy, kernel_spectrum):
    cb = jnp.asarray(two_parts(matrices()))
    tw = jnp.asarray(twiddles())
    V = pltpu.VMEM
    D = pltpu.SemaphoreType.DMA
    block = (3, 128, 256)
    band = (3, 16, 2048)
    slots = (3, 512, 128)
    doubled = pl.pallas_call(
        functools.partial(kernel, sizes),
        out_shape=jax.ShapeDtypeStruct(block, F32),
        in_specs=[pl.BlockSpec(memory_space=pl.ANY)] * 5,
        out_specs=pl.BlockSpec(memory_space=pltpu.VMEM),
        scratch_shapes=[
            V(block, F32), V((128, 256), jnp.int32), V((4, 24, 4096), F32), V((2, N_TABLES, 256, 256), BF16),
            V((544, 128), F32),
            V(block, F32), V((2,) + band, F32), V(band, F32), V(band, F32), V(band, F32),
            V(band, F32), V((2, 2, 8, 2048), F32), V((4, 2, 256, 128), F32),
            V((4, 16, 256), F32), V((4, 16, 256), F32), V((4, 256, 128), F32),
            V(slots, F32), V(slots, F32), V(slots, F32), V(slots, F32),
            V((2, 3, 256, 256), BF16), V((2, 256, 256), F32), V((2, 256, 256), BF16), V((2, 2, 256, 256), BF16),
            V((3, 256, 256), F32), V((3, 16, 256), F32), V((128, 128), F32),
            D((5,)), D, D((3,)), D((2,)), D((2, 2)), D, D, D, D((3,)), D, D((3,)), D, D,
            pltpu.SemaphoreType.REGULAR,
        ],
        compiler_params=pltpu.CompilerParams(
            collective_id=0, has_side_effects=True, vmem_limit_bytes=56 * 1024 * 1024
        ),
    )(mag, occupancy, kernel_spectrum, cb, tw)
    late, doubled = lax.optimization_barrier((occupancy, doubled))
    occ = late.astype(F32)
    mean_rate = 0.5 * doubled
    v = [mag[m] * occ + TIME_STEP * mean_rate[m] for m in range(3)]
    root = jnp.sqrt(squared(v) + 1.0 - occ)
    return jnp.stack([c / root for c in v]), mean_rate


def solution(mesh):
    n_tx, n_ty = mesh.shape["tx"], mesh.shape["ty"]
    side = math.isqrt(n_tx)
    return jax.shard_map(
        functools.partial(body, (side, side, n_ty // 2)),
        mesh=mesh,
        in_specs=(P(None, "tx", "ty"), P("tx", "ty"), P(None, ("tx", "ty"), None)),
        out_specs=(P(None, "tx", "ty"), P(None, "tx", "ty")),
        check_vma=False,
    )
```

```python
import functools
import itertools
import math

import jax
import jax.numpy as jnp
import ml_dtypes
import numpy as np
from jax import lax
from jax.experimental import pallas as pl
from jax.experimental.pallas import tpu as pltpu
from jax.sharding import PartitionSpec as P

DAMPING = 0.3
STIFFNESS = 0.25
TIME_STEP = 0.25
MESH = pl.DeviceIdType.MESH
F32 = jnp.float32
BF16 = jnp.bfloat16


(T_WA, T_WAQ, T_W1R, T_W1I, T_W2, T_W2I, T_BR, T_BI, T_W3, T_W3Q, T_SF, T_SI) = range(12)
N_TABLES = 12


def angle(left, right, length):
    product = np.arange(left)[:, None] * np.arange(right)[None, :] % length
    return 2.0 * math.pi * product / length


def matrices():
    out = np.zeros((N_TABLES, 256, 256))
    th = angle(128, 128, 128)
    cos, sin = np.cos(th), np.sin(th)
    out[T_WA] = np.block([[cos, sin], [-sin, cos]])
    scale = -(2.0**-24)
    out[T_W3] = 2.0 * scale * np.block([[cos, sin], [-sin, cos]])
    ph = th + 2.0 * math.pi * np.arange(128)[None, :] / 256.0
    low, high = np.arange(1, 64), np.arange(64, 128)
    sign = 1.0 - 2.0 * (np.arange(128) % 2)
    q = np.zeros((2, 128, 2, 128))
    q[0, 0, 0], q[1, 0, 0] = 1.0, sign
    q[0, low, 0], q[1, low, 0] = cos[low], -sin[low]
    q[0, high, 1], q[1, high, 1] = np.cos(ph)[high], -np.sin(ph)[high]
    out[T_WAQ] = q.reshape(256, 256)
    weight = np.full((128, 1, 1), 2.0)
    weight[0] = 1.0
    out[T_W3Q] = scale * (q * weight).reshape(256, 256)
    th = angle(256, 128, 256)
    cos, sin = np.cos(th), np.sin(th)
    out[T_W1R] = np.concatenate([cos, sin], 1)
    out[T_W1I] = np.concatenate([-sin, cos], 1)
    out[T_BR] = np.concatenate([cos.T, sin.T], 0)
    out[T_BI] = np.concatenate([-sin.T, cos.T], 0)
    th = angle(16, 16, 16)
    cos, sin = np.cos(th), np.sin(th)
    eight = np.eye(8)
    wc = np.einsum("ab,id->aidb", eight, cos).reshape(128, 128)
    ws = np.einsum("ab,id->aidb", eight, sin).reshape(128, 128)
    out[T_W2] = np.block([[wc, -ws], [ws, wc]])
    out[T_W2I] = np.block([[wc.T, ws.T], [-ws.T, wc.T]])
    four = np.eye(4)
    sc = np.kron(four, cos)
    ss = np.kron(four, sin)
    none = np.zeros((64, 64))
    out[T_SF, :, :128] = np.block([[sc, -ss], [none, none], [ss, sc], [none, none]])
    out[T_SI, :128, :128] = np.block([[sc.T, ss.T], [-ss.T, sc.T]])
    return out


def two_parts(value):
    high = value.astype(np.float32).astype(ml_dtypes.bfloat16)
    low = (value - high.astype(np.float64)).astype(np.float32).astype(ml_dtypes.bfloat16)
    both = np.stack([high, low])
    for k in (T_SF, T_SI):
        both[0, k, :, 128:] = low[k, :, :128]
    both[0, T_SI, 128:, :128] = high[T_SI, :128, :128]
    return both


def twiddles():
    th = 2.0 * math.pi * (np.arange(256)[:, None] * (np.arange(128) % 16)[None, :]) / 4096.0
    ty = angle(16, 128, 4096)
    return np.concatenate([np.cos(th), np.sin(th), np.cos(ty), np.sin(ty)], 0).astype(np.float32)


def split(value):
    high = value.astype(BF16)
    return high, (value - high.astype(F32)).astype(BF16)


def product(a, b, form=(((1,), (0,)), ((), ()))):
    dot = functools.partial(lax.dot_general, dimension_numbers=form, preferred_element_type=F32)
    return dot(a[0], b[0]) + (dot(a[0], b[1]) + dot(a[1], b[0]))


LANES = (((1,), (1,)), ((), ()))


def cross(left, right):
    return [
        left[1] * right[2] - left[2] * right[1],
        left[2] * right[0] - left[0] * right[2],
        left[0] * right[1] - left[1] * right[0],
    ]


def squared(v):
    return v[0] * v[0] + v[1] * v[1] + v[2] * v[2]


def far_first(n_x, n_y, n_z):
    def far(o):
        return sum(min(d, k - d) for d, k in zip(o, (n_x, n_y, n_z)))

    offsets = [o for o in itertools.product(range(n_x), range(n_y), range(n_z), range(2)) if any(o)]
    mixed = np.random.RandomState(1).permutation(len(offsets))
    return sorted((offsets[k] for k in mixed), key=lambda o: -far(o))


def kernel(sizes, mag_h, occ_h, ks_h, cb_h, tw_h, out_ref, mag, occ, ks, cb, tw, m0l, fb, k1, dm, ex,
           mr, hb, kt, kr, kr2, kst, s1, r1, s2, r2, u, zb, xs, ys, pb, pq, os, load_sem, ty_send, ty_recv,
           h_send, h_recv, k_send, k_recv, a_send, a_recv, b_send, b_recv, f_send, f_recv, ready):
    n_x, n_y, n_z = sizes
    n_ty = 2 * n_z
    n = n_x * n_y * n_ty
    tx, ty = lax.axis_index("tx"), lax.axis_index("ty")
    me = tx * n_ty + ty
    px, py, pz, pc = tx // n_y, lax.rem(tx, n_y), ty // 2, lax.rem(ty, 2)
    at_x = [lax.rem(px + d, n_x) * n_y for d in range(n_x)]
    at_y = [lax.rem(py + d, n_y) for d in range(n_y)]
    at_z = [lax.rem(pz + d, n_z) * 2 for d in range(n_z)]
    at_c = [pc, 1 - pc]
    others = far_first(n_x, n_y, n_z)

    loads = [
        pltpu.make_async_copy(mag_h, mag, load_sem.at[0]),
        pltpu.make_async_copy(occ_h, occ, load_sem.at[1]),
        pltpu.make_async_copy(ks_h.at[:, pl.ds(0, 24), :], ks, load_sem.at[2]),
        pltpu.make_async_copy(cb_h, cb, load_sem.at[3]),
        pltpu.make_async_copy(tw_h, tw, load_sem.at[4]),
    ]
    for k in (0, 1, 4, 3, 2):
        loads[k].start()

    barrier = pltpu.get_barrier_semaphore()
    line = [o for o in others if o[:2] == (0, 0)]
    plane = [o for o in others if o[2:] == (0, 0)]
    for dx, dy, dz, dc in plane + line:
        to = (at_x[dx] + at_y[dy], at_z[dz] + at_c[dc])
        pl.semaphore_signal(barrier, inc=1, device_id=to, device_id_type=MESH)
    loads[0].wait()
    loads[1].wait()
    occf = occ[...].astype(F32)
    for m in range(3):
        m0l[m] = mag[m] * occf
    pl.semaphore_wait(barrier, len(plane) + len(line))

    def table(k):
        return cb[0, k], cb[1, k]

    mine = pl.ds(pl.multiple_of(ty * 256, 256), 256)
    own_rows = pl.ds(pl.multiple_of(ty * 16, 16), 16)
    for m in (2, 0, 1):
        for _, _, dz, dc in line:
            to = at_z[dz] + at_c[dc]
            pltpu.make_async_remote_copy(
                src_ref=m0l.at[m, pl.ds(pl.multiple_of(to * 16, 16), 16), :], dst_ref=fb.at[0, m, :, mine],
                send_sem=ty_send, recv_sem=ty_recv.at[m], device_id=(tx, to), device_id_type=MESH,
            ).start()
        pltpu.make_async_copy(m0l.at[m, own_rows, :], fb.at[0, m, :, mine], ty_recv.at[m]).start()

    for _, _, dz, dc in line:
        pl.semaphore_signal(ready, inc=1, device_id=(tx, at_z[dz] + at_c[dc]), device_id_type=MESH)
    loads[3].wait()
    loads[4].wait()
    pl.semaphore_wait(ready, len(line))
    own = pl.ds(pl.multiple_of(me * 4, 4), 4)

    def exchange(m, source, target, send, recv):
        for dx, dy, dz, dc in others:
            a, b = at_x[dx] + at_y[dy], at_z[dz] + at_c[dc]
            there = pl.ds(pl.multiple_of((a * n_ty + b) * 4, 4), 4)
            pltpu.make_async_remote_copy(
                src_ref=source.at[m, there, :], dst_ref=target.at[m, own, :],
                send_sem=send, recv_sem=recv.at[m], device_id=(a, b), device_id_type=MESH,
            ).start()
        pltpu.make_async_copy(source.at[m, own, :], target.at[m, own, :], recv.at[m]).start()

    def arrived(m, target, recv):
        pltpu.make_async_copy(target.at[m], target.at[m], recv.at[m]).wait()

    def sent(source, send):
        rest = source.at[:, pl.ds(0, 4 * (n - 1)), :]
        pltpu.make_async_copy(rest, rest, send).wait()

    lane = lax.broadcasted_iota(jnp.int32, (128, 128), 1)
    after, before = lax.rem(me + 1, n), lax.rem(me + n - 1, n)

    def row_copy():
        return pltpu.make_async_remote_copy(
            src_ref=kr, dst_ref=kr2, send_sem=k_send, recv_sem=k_recv, device_id=(0, 0), device_id_type=MESH
        )

    def kernel_tables():
        loads[2].wait()
        upper = me >= n // 2
        top = lax.broadcasted_iota(jnp.int32, (8, 256), 0) == 0
        for k in range(4):
            for d in range(16):
                kr[k, pl.ds(d, 1), :] = ks[k, pl.ds(0, 1), pl.ds(256 * d, 256)]

        @pl.when(me == n // 2)
        def _():
            row_copy().start()

        for k in range(4):
            for h in range(2):
                tiles = []
                for d in range(16):
                    tile = ks[k, pl.ds(8 * h, 8), pl.ds(256 * d, 256)]
                    if h == 0:
                        other = ks[k, pl.ds(16, 8), pl.ds(256 * d, 256)]
                        tile = jnp.where(jnp.logical_and(top, upper), other, tile)
                    tiles.append(tile)
                kt[k, h] = jnp.concatenate(tiles, 0).T

        @pl.when(me == n // 2)
        def _():
            row_copy().wait_send()

        @pl.when(me == 0)
        def _():
            row_copy().wait_recv()
            def both(k):
                return jnp.concatenate([kr[k], kr2[k]], 0)

            kst[0] = jnp.concatenate([both(0), both(1)] * 2, 0).T
            kst[1] = jnp.concatenate([both(3)] * 4, 0).T
            kst[2] = jnp.concatenate([both(2)] * 4, 0).T

    def step(it, _):
        def place(m, c):
            if isinstance(m, int) and m == 2:
                return 0, 16 * c
            return 1 + c // 8, pl.multiple_of(128 * m + 16 * (c % 8), 16)

        def y_first(m, _):
            @pl.when(it == 0)
            def _():
                arrived(m, fb.at[0], ty_recv)

            a = [fb[it, m, :, pl.ds(128 * k, 128)] for k in range(16)]
            real, imag = [None] * 17, [None] * 17
            for c in range(9):
                sums = []
                for odd in range(2):
                    re, im = None, None
                    for k in range(odd, 16, 2):
                        w = 2.0 * math.pi * (c * k % 32) / 32.0
                        wr, wi = round(math.cos(w), 15), round(-math.sin(w), 15)
                        if wr != 0.0:
                            re = a[k] * wr if re is None else re + a[k] * wr
                        if wi != 0.0:
                            im = a[k] * wi if im is None else im + a[k] * wi
                    zero = jnp.zeros_like(a[0])
                    sums.append((zero if re is None else re, zero if im is None else im))
                (er, ei), (ro, io) = sums
                real[c], imag[c] = er + ro, ei + io
                real[16 - c], imag[16 - c] = er - ro, io - ei
            for c in range(16):
                if c == 0:
                    vr, vi = real[0], real[16]
                else:
                    cos, sin = tw[pl.ds(512 + c, 1), :], tw[pl.ds(528 + c, 1), :]
                    vr, vi = real[c] * cos + imag[c] * sin, imag[c] * cos - real[c] * sin
                chunk, start = place(m, c)
                for part, v in enumerate((vr, vi)):
                    for k, piece in enumerate(split(v)):
                        u[k, chunk, pl.ds(start, 16), pl.ds(128 * part, 128)] = piece
            return 0

        def y_second(g, _):
            full = product(table(T_WA), (u[0, g], u[1, g]), LANES)
            first = product(table(T_WAQ), (u[0, g], u[1, g]), LANES)
            for part in range(2):
                for b in range(2):
                    block = (slice(128 * part, 128 * part + 128), slice(128 * b, 128 * b + 128))
                    inside = jnp.logical_and(lane < 16, g == 1 if b else g < 2)
                    s1[g, pl.ds(2 * part + b, 128, stride=4), :] = jnp.where(inside, first[block], full[block])
            exchange(g, s1, r1, a_send, a_recv)
            return 0

        @pl.when(it == 1)
        def _():
            sent(s1, a_send)
            sent(s2, b_send)

        y_first(2, 0)
        y_second(0, 0)
        lax.fori_loop(0, 2, y_first, 0)
        lax.fori_loop(1, 3, y_second, 0)

        halos = []
        for side, (to, row) in enumerate(((after, 15), (before, 0))):
            halos.append(pltpu.make_async_remote_copy(
                src_ref=fb.at[it, :, row], dst_ref=hb.at[it, side, pl.ds(0, 3)],
                send_sem=h_send.at[side], recv_sem=h_recv.at[it, side],
                device_id=(to // n_ty, lax.rem(to, n_ty)), device_id_type=MESH,
            ))
        for halo in halos:
            halo.start()

        @pl.when(it == 0)
        def _():
            kernel_tables()

        def mirrored_rows(g, group):
            dot = functools.partial(jnp.dot, preferred_element_type=F32)
            halves = lambda v: v[:, :128] + v[:, 128:]
            cos, sin = tw[pl.ds(0, 256), :], tw[pl.ds(256, 256), :]
            seq = jnp.zeros((128, 128), F32)
            for j in range(2):
                for b in range(len(group)):
                    block = r1[g, pl.ds(2 * j + b, 128, stride=4), :]
                    at = 32 * b + 16 * j
                    inside = jnp.logical_and(lane >= at, lane < at + 16)
                    seq = jnp.where(inside, pltpu.roll(block, at, 1) if at else block, seq)
            xh, xl = split(seq)
            x = jnp.concatenate([
                jnp.concatenate([xh, xl], 1), jnp.concatenate([jnp.zeros_like(xh), xh], 1)], 0)
            ar, ai = [
                halves(dot(jnp.concatenate([cb[0, k, :, pl.ds(0, 128)], cb[1, k, :, pl.ds(0, 128)]], 1), x))
                for k in (T_W1R, T_W1I)
            ]
            vh, vl = split(jnp.concatenate([ar * cos + ai * sin, ai * cos - ar * sin], 1))
            z = halves(dot(vh, cb[0, T_SF])) + dot(vl, cb[0, T_SF, :, pl.ds(0, 128)])
            wide = lax.broadcasted_iota(jnp.int32, (256, 128), 1)
            if len(group) == 1:
                field = kst[2] * z
            else:
                swapped = jnp.where(lax.rem(wide // 32, 2) == 0, pltpu.roll(z, 96, 1), pltpu.roll(z, 32, 1))
                field = kst[0] * z + kst[1] * swapped
            back = halves(dot(jnp.concatenate(split(field), 1), cb[0, T_SI]))
            turned = pltpu.roll(back, 64, 1) * sin
            yh, yl = split(back * cos + jnp.where(wide < 64, -turned, turned))
            y = jnp.concatenate([yh, yl], 1)
            re, im = [
                halves(dot(cb[0, k, pl.ds(0, 128), :], y)) + dot(cb[1, k, pl.ds(0, 128), :], yh)
                for k in (T_BR, T_BI)
            ]
            os[...] = re + pltpu.roll(im, 64, 1)

        def x_chunk(g, group):
            arrived(g, r1, a_recv)
            for part in range(2):
                for b in range(2):
                    block = r1[g, pl.ds(2 * part + b, 128, stride=4), :]
                    for k, piece in enumerate(split(block)):
                        xs[k, pl.ds(128 * part, 128), pl.ds(128 * b, 128)] = piece
            x = (xs[0], xs[1])
            tr, ti = product(table(T_W1R), x), product(table(T_W1I), x)
            cos, sin = tw[pl.ds(0, 256), :], tw[pl.ds(256, 256), :]
            for b in range(2):
                ar, ai = tr[:, 128 * b:128 * b + 128], ti[:, 128 * b:128 * b + 128]
                v = jnp.concatenate([ar * cos + ai * sin, ai * cos - ar * sin], 1)
                zb[b] = product(split(v), table(T_W2))

            mirrored = me == 0 if len(group) == 1 else jnp.logical_and(me == 0, g == 1)

            @pl.when(mirrored)
            def _():
                mirrored_rows(g, group)

            for b in range(2):
                pieces = []
                for part in range(2):
                    cols = pl.ds(128 * part, 128)
                    if len(group) == 1:
                        pieces.append(kt[2, b] * zb[b, :, cols])
                    else:
                        pieces.append(kt[b, g - 1] * zb[b, :, cols] + kt[3, g - 1] * zb[1 - b, :, cols])
                p = product(split(jnp.concatenate(pieces, 1)), table(T_W2I))
                pr, pi = p[:, :128], p[:, 128:]
                for part, v in enumerate((pr * cos - pi * sin, pi * cos + pr * sin)):
                    for k, piece in enumerate(split(v)):
                        ys[k, part, :, pl.ds(128 * b, 128)] = piece
            o = product(table(T_BR), (ys[0, 0], ys[1, 0])) + product(table(T_BI), (ys[0, 1], ys[1, 1]))
            for part in range(2):
                for b in range(2):
                    s2[g, pl.ds(2 * part + b, 128, stride=4), :] = (
                        o[128 * part:128 * part + 128, 128 * b:128 * b + 128])

            @pl.when(mirrored)
            def _():
                for j in range(2):
                    for b in range(len(group)):
                        rows = pl.ds(2 * j + b, 128, stride=4)
                        shift = (128 - 32 * b - 16 * j) % 128
                        moved = pltpu.roll(os[...], shift, 1) if shift else os[...]
                        s2[g, rows, :] = jnp.where(lane < 16, moved, s2[g, rows, :])

            exchange(g, s2, r2, b_send, b_recv)

        def xy_chunk(g, _):
            x_chunk(g, (0, 1))
            return 0

        x_chunk(0, (2,))
        lax.fori_loop(1, 3, xy_chunk, 0)

        for halo in halos:
            halo.wait_recv()
        row = lax.broadcasted_iota(jnp.int32, (16, 2048), 0)
        col = lax.broadcasted_iota(jnp.int32, (16, 2048), 1)
        for m in range(3):
            f = fb[it, m]
            low = jnp.where(me > 0, hb[it, 0, pl.ds(m, 1), :], 0.0)
            high = jnp.where(me < n - 1, hb[it, 1, pl.ds(m, 1), :], 0.0)
            up = jnp.where(row == 0, low, pltpu.roll(f, 1, 0))
            down = jnp.where(row == 15, high, pltpu.roll(f, 15, 0))
            left = jnp.where(col == 0, 0.0, pltpu.roll(f, 1, 1))
            right = jnp.where(col == 2047, 0.0, pltpu.roll(f, 2047, 1))
            ex[m] = STIFFNESS * (down + up + right + left)
        for halo in halos:
            halo.wait_send()

        def y_inverse_first(g, _):
            arrived(g, r2, b_recv)
            for part in range(2):
                for b in range(2):
                    block = r2[g, pl.ds(2 * part + b, 128, stride=4), :].T
                    for k, piece in enumerate(split(block)):
                        xs[k, pl.ds(128 * b, 128), pl.ds(128 * part, 128)] = piece
            pb[g] = product((xs[0], xs[1]), table(T_W3))

            def ends(m, row):
                rows = pl.ds(row, 16)
                pq[m] = product((xs[0, rows, :], xs[1, rows, :]), table(T_W3Q))

            if isinstance(g, int):
                ends(2, 0)
            else:
                @pl.when(g == 1)
                def _():
                    ends(0, 0)
                    ends(1, 128)

            return 0

        def y_inverse_second(m, _):
            real, imag = [None] * 16, [None] * 16
            for c in range(1, 16):
                cos, sin = tw[pl.ds(512 + c, 1), :], tw[pl.ds(528 + c, 1), :]
                chunk, start = place(m, c)
                br, bi = pb[chunk, pl.ds(start, 16), pl.ds(0, 128)], pb[chunk, pl.ds(start, 16), pl.ds(128, 128)]
                real[c], imag[c] = br * cos - bi * sin, bi * cos + br * sin
            even, odd_part = pq[m, :, pl.ds(0, 128)], pq[m, :, pl.ds(128, 128)]
            ends = (even + odd_part, even - odd_part)
            pairs = []
            for odd in range(2):
                pairs.append([
                    (real[c] - real[16 - c], imag[c] + imag[16 - c]) if odd
                    else (real[c] + real[16 - c], imag[c] - imag[16 - c]) for c in range(1, 8)
                ])
            for a in range(16):
                total = ends[a % 2]
                for c in range(1, 9):
                    re, im = pairs[a % 2][c - 1] if c < 8 else (real[8], imag[8])
                    w = 2.0 * math.pi * (c * a % 32) / 32.0
                    wr, wi = round(math.cos(w), 15), round(math.sin(w), 15)
                    if wr != 0.0:
                        total = total + re * wr
                    if wi != 0.0:
                        total = total - im * wi
                dm[m, :, pl.ds(128 * a, 128)] = total
            return 0

        y_inverse_first(0, 0)
        y_inverse_second(2, 0)
        lax.fori_loop(1, 3, y_inverse_first, 0)
        lax.fori_loop(0, 2, y_inverse_second, 0)

        def advance(j, _):
            far = j // 2
            dz = jnp.where(far == 0, 2, jnp.where(far == 1, 1, jnp.where(far == 2, 3, 0)))
            to = lax.rem(pz + dz, n_z) * 2 + lax.rem(pc + j + 1, 2)
            cols = pl.ds(pl.multiple_of(to * 256, 256), 256)
            m0 = [fb[0, m, :, cols] for m in range(3)]
            f = [fb[it, m, :, cols] for m in range(3)]
            heff = [dm[m, :, cols] + ex[m, :, cols] for m in range(3)]
            torque = cross(f, heff)
            damped = cross(f, torque)
            rate = [(t + DAMPING * d) * (-1.0 / (1.0 + DAMPING * DAMPING)) for t, d in zip(torque, damped)]

            @pl.when(it == 0)
            def _():
                filled = jnp.where(squared(m0) > 0.5, 0.0, 1.0)
                v = [m + TIME_STEP * r for m, r in zip(m0, rate)]
                root = jnp.sqrt(squared(v) + filled)
                for m in range(3):
                    k1[m, :, cols] = rate[m]
                    fb[1, m, :, cols] = v[m] / root

            @pl.when(it == 1)
            def _():
                along = rate[0] * m0[0] + rate[1] * m0[1] + rate[2] * m0[2]
                for m in range(3):
                    mr[m, :, cols] = k1[m, :, cols] + (rate[m] - along * m0[m])

                @pl.when(j < n_ty - 1)
                def _():
                    pltpu.make_async_remote_copy(
                        src_ref=mr.at[:, :, cols], dst_ref=out_ref.at[:, own_rows, :],
                        send_sem=f_send, recv_sem=f_recv, device_id=(tx, to), device_id_type=MESH,
                    ).start()

                @pl.when(j == n_ty - 1)
                def _():
                    pltpu.make_async_copy(mr.at[:, :, cols], out_ref.at[:, own_rows, :], f_recv).start()

            return 0

        lax.fori_loop(0, n_ty, advance, 0)
        return 0

    lax.fori_loop(0, 2, step, 0)
    rest = m0l.at[:, pl.ds(0, 16 * (n_ty - 1)), :]
    pltpu.make_async_copy(rest, rest, ty_send).wait()
    sent(s1, a_send)
    sent(s2, b_send)
    pltpu.make_async_copy(out_ref, out_ref, f_recv).wait()
    pltpu.make_async_copy(rest, rest, f_send).wait()


def body(sizes, mag, occupancy, kernel_spectrum):
    cb = jnp.asarray(two_parts(matrices()))
    tw = jnp.asarray(twiddles())
    V = pltpu.VMEM
    D = pltpu.SemaphoreType.DMA
    block = (3, 128, 256)
    band = (3, 16, 2048)
    slots = (3, 512, 128)
    doubled = pl.pallas_call(
        functools.partial(kernel, sizes),
        out_shape=jax.ShapeDtypeStruct(block, F32),
        in_specs=[pl.BlockSpec(memory_space=pl.ANY)] * 5,
        out_specs=pl.BlockSpec(memory_space=pltpu.VMEM),
        scratch_shapes=[
            V(block, F32), V((128, 256), jnp.int32), V((4, 24, 4096), F32), V((2, N_TABLES, 256, 256), BF16),
            V((544, 128), F32),
            V(block, F32), V((2,) + band, F32), V(band, F32), V(band, F32), V(band, F32),
            V(band, F32), V((2, 2, 8, 2048), F32), V((4, 2, 256, 128), F32),
            V((4, 16, 256), F32), V((4, 16, 256), F32), V((3, 256, 128), F32),
            V(slots, F32), V(slots, F32), V(slots, F32), V(slots, F32),
            V((2, 3, 256, 256), BF16), V((2, 256, 256), F32), V((2, 256, 256), BF16), V((2, 2, 256, 256), BF16),
            V((3, 256, 256), F32), V((3, 16, 256), F32), V((128, 128), F32),
            D((5,)), D, D((3,)), D((2,)), D((2, 2)), D, D, D, D((3,)), D, D((3,)), D, D,
            pltpu.SemaphoreType.REGULAR,
        ],
        compiler_params=pltpu.CompilerParams(
            collective_id=0, has_side_effects=True, vmem_limit_bytes=56 * 1024 * 1024
        ),
    )(mag, occupancy, kernel_spectrum, cb, tw)
    late, doubled = lax.optimization_barrier((occupancy, doubled))
    occ = late.astype(F32)
    mean_rate = 0.5 * doubled
    v = [mag[m] * occ + TIME_STEP * mean_rate[m] for m in range(3)]
    root = jnp.sqrt(squared(v) + 1.0 - occ)
    return jnp.stack([c / root for c in v]), mean_rate


def solution(mesh):
    n_tx, n_ty = mesh.shape["tx"], mesh.shape["ty"]
    side = math.isqrt(n_tx)
    return jax.shard_map(
        functools.partial(body, (side, side, n_ty // 2)),
        mesh=mesh,
        in_specs=(P(None, "tx", "ty"), P("tx", "ty"), P(None, ("tx", "ty"), None)),
        out_specs=(P(None, "tx", "ty"), P(None, "tx", "ty")),
        check_vma=False,
    )
```

```python
import functools
import itertools
import math

import jax
import jax.numpy as jnp
import ml_dtypes
import numpy as np
from jax import lax
from jax.experimental import pallas as pl
from jax.experimental.pallas import tpu as pltpu
from jax.sharding import PartitionSpec as P

DAMPING = 0.3
STIFFNESS = 0.25
TIME_STEP = 0.25
MESH = pl.DeviceIdType.MESH
F32 = jnp.float32
BF16 = jnp.bfloat16


(T_WA, T_WAQ, T_W1R, T_W1I, T_W2, T_W2I, T_BR, T_BI, T_W3, T_W3Q, T_SF, T_SI) = range(12)
N_TABLES = 12


def angle(left, right, length):
    product = np.arange(left)[:, None] * np.arange(right)[None, :] % length
    return 2.0 * math.pi * product / length


def matrices():
    out = np.zeros((N_TABLES, 256, 256))
    th = angle(128, 128, 128)
    cos, sin = np.cos(th), np.sin(th)
    out[T_WA] = np.block([[cos, sin], [-sin, cos]])
    scale = -(2.0**-24)
    out[T_W3] = 2.0 * scale * np.block([[cos, sin], [-sin, cos]])
    ph = th + 2.0 * math.pi * np.arange(128)[None, :] / 256.0
    low, high = np.arange(1, 64), np.arange(64, 128)
    sign = 1.0 - 2.0 * (np.arange(128) % 2)
    q = np.zeros((2, 128, 2, 128))
    q[0, 0, 0], q[1, 0, 0] = 1.0, sign
    q[0, low, 0], q[1, low, 0] = cos[low], -sin[low]
    q[0, high, 1], q[1, high, 1] = np.cos(ph)[high], -np.sin(ph)[high]
    out[T_WAQ] = q.reshape(256, 256)
    weight = np.full((128, 1, 1), 2.0)
    weight[0] = 1.0
    out[T_W3Q] = scale * (q * weight).reshape(256, 256)
    th = angle(256, 128, 256)
    cos, sin = np.cos(th), np.sin(th)
    out[T_W1R] = np.concatenate([cos, sin], 1)
    out[T_W1I] = np.concatenate([-sin, cos], 1)
    out[T_BR] = np.concatenate([cos.T, sin.T], 0)
    out[T_BI] = np.concatenate([-sin.T, cos.T], 0)
    th = angle(16, 16, 16)
    cos, sin = np.cos(th), np.sin(th)
    eight = np.eye(8)
    wc = np.einsum("ab,id->aidb", eight, cos).reshape(128, 128)
    ws = np.einsum("ab,id->aidb", eight, sin).reshape(128, 128)
    out[T_W2] = np.block([[wc, -ws], [ws, wc]])
    out[T_W2I] = np.block([[wc.T, ws.T], [-ws.T, wc.T]])
    four = np.eye(4)
    sc = np.kron(four, cos)
    ss = np.kron(four, sin)
    none = np.zeros((64, 64))
    out[T_SF, :, :128] = np.block([[sc, -ss], [none, none], [ss, sc], [none, none]])
    out[T_SI, :128, :128] = np.block([[sc.T, ss.T], [-ss.T, sc.T]])
    return out


def two_parts(value):
    high = value.astype(np.float32).astype(ml_dtypes.bfloat16)
    low = (value - high.astype(np.float64)).astype(np.float32).astype(ml_dtypes.bfloat16)
    both = np.stack([high, low])
    for k in (T_SF, T_SI):
        both[0, k, :, 128:] = low[k, :, :128]
    both[0, T_SI, 128:, :128] = high[T_SI, :128, :128]
    return both


def twiddles():
    th = 2.0 * math.pi * (np.arange(256)[:, None] * (np.arange(128) % 16)[None, :]) / 4096.0
    ty = angle(16, 128, 4096)
    return np.concatenate([np.cos(th), np.sin(th), np.cos(ty), np.sin(ty)], 0).astype(np.float32)


def split(value):
    high = value.astype(BF16)
    return high, (value - high.astype(F32)).astype(BF16)


def product(a, b, form=(((1,), (0,)), ((), ()))):
    dot = functools.partial(lax.dot_general, dimension_numbers=form, preferred_element_type=F32)
    return dot(a[0], b[0]) + (dot(a[0], b[1]) + dot(a[1], b[0]))


LANES = (((1,), (1,)), ((), ()))


def cross(left, right):
    return [
        left[1] * right[2] - left[2] * right[1],
        left[2] * right[0] - left[0] * right[2],
        left[0] * right[1] - left[1] * right[0],
    ]


def squared(v):
    return v[0] * v[0] + v[1] * v[1] + v[2] * v[2]


def far_first(n_x, n_y, n_z):
    def far(o):
        return sum(min(d, k - d) for d, k in zip(o, (n_x, n_y, n_z)))

    offsets = [o for o in itertools.product(range(n_x), range(n_y), range(n_z), range(2)) if any(o)]
    mixed = np.random.RandomState(1).permutation(len(offsets))
    return sorted((offsets[k] for k in mixed), key=lambda o: -far(o))


def kernel(sizes, mag_h, occ_h, ks_h, cb_h, tw_h, out_ref, mag, occ, ks, cb, tw, m0l, fb, k1, dm, ex,
           mr, hb, kt, kr, kr2, kst, s1, r1, s2, r2, u, zb, xs, ys, pb, pq, load_sem, ty_send, ty_recv,
           h_send, h_recv, k_send, k_recv, a_send, a_recv, b_send, b_recv, f_send, f_recv, ready):
    n_x, n_y, n_z = sizes
    n_ty = 2 * n_z
    n = n_x * n_y * n_ty
    tx, ty = lax.axis_index("tx"), lax.axis_index("ty")
    me = tx * n_ty + ty
    px, py, pz, pc = tx // n_y, lax.rem(tx, n_y), ty // 2, lax.rem(ty, 2)
    at_x = [lax.rem(px + d, n_x) * n_y for d in range(n_x)]
    at_y = [lax.rem(py + d, n_y) for d in range(n_y)]
    at_z = [lax.rem(pz + d, n_z) * 2 for d in range(n_z)]
    at_c = [pc, 1 - pc]
    others = far_first(n_x, n_y, n_z)

    loads = [
        pltpu.make_async_copy(mag_h, mag, load_sem.at[0]),
        pltpu.make_async_copy(occ_h, occ, load_sem.at[1]),
        pltpu.make_async_copy(ks_h.at[:, pl.ds(0, 24), :], ks, load_sem.at[2]),
        pltpu.make_async_copy(cb_h, cb, load_sem.at[3]),
        pltpu.make_async_copy(tw_h, tw, load_sem.at[4]),
    ]
    for k in (0, 1, 4, 3, 2):
        loads[k].start()

    barrier = pltpu.get_barrier_semaphore()
    line = [o for o in others if o[:2] == (0, 0)]
    plane = [o for o in others if o[2:] == (0, 0)]
    for dx, dy, dz, dc in plane + line:
        to = (at_x[dx] + at_y[dy], at_z[dz] + at_c[dc])
        pl.semaphore_signal(barrier, inc=1, device_id=to, device_id_type=MESH)
    loads[0].wait()
    loads[1].wait()
    occf = occ[...].astype(F32)
    for m in range(3):
        m0l[m] = mag[m] * occf
    pl.semaphore_wait(barrier, len(plane) + len(line))

    def table(k):
        return cb[0, k], cb[1, k]

    mine = pl.ds(pl.multiple_of(ty * 256, 256), 256)
    own_rows = pl.ds(pl.multiple_of(ty * 16, 16), 16)
    for m in (2, 0, 1):
        for _, _, dz, dc in line:
            to = at_z[dz] + at_c[dc]
            pltpu.make_async_remote_copy(
                src_ref=m0l.at[m, pl.ds(pl.multiple_of(to * 16, 16), 16), :], dst_ref=fb.at[0, m, :, mine],
                send_sem=ty_send, recv_sem=ty_recv.at[m], device_id=(tx, to), device_id_type=MESH,
            ).start()
        pltpu.make_async_copy(m0l.at[m, own_rows, :], fb.at[0, m, :, mine], ty_recv.at[m]).start()

    for _, _, dz, dc in line:
        pl.semaphore_signal(ready, inc=1, device_id=(tx, at_z[dz] + at_c[dc]), device_id_type=MESH)
    loads[3].wait()
    loads[4].wait()
    pl.semaphore_wait(ready, len(line))
    own = pl.ds(pl.multiple_of(me * 4, 4), 4)

    def exchange(m, source, target, send, recv):
        for dx, dy, dz, dc in others:
            a, b = at_x[dx] + at_y[dy], at_z[dz] + at_c[dc]
            there = pl.ds(pl.multiple_of((a * n_ty + b) * 4, 4), 4)
            pltpu.make_async_remote_copy(
                src_ref=source.at[m, there, :], dst_ref=target.at[m, own, :],
                send_sem=send, recv_sem=recv.at[m], device_id=(a, b), device_id_type=MESH,
            ).start()
        pltpu.make_async_copy(source.at[m, own, :], target.at[m, own, :], recv.at[m]).start()

    def arrived(m, target, recv):
        pltpu.make_async_copy(target.at[m], target.at[m], recv.at[m]).wait()

    def sent(source, send):
        rest = source.at[:, pl.ds(0, 4 * (n - 1)), :]
        pltpu.make_async_copy(rest, rest, send).wait()

    lane = lax.broadcasted_iota(jnp.int32, (128, 128), 1)
    after, before = lax.rem(me + 1, n), lax.rem(me + n - 1, n)

    def row_copy():
        return pltpu.make_async_remote_copy(
            src_ref=kr, dst_ref=kr2, send_sem=k_send, recv_sem=k_recv, device_id=(0, 0), device_id_type=MESH
        )

    def kernel_tables():
        loads[2].wait()
        upper = me >= n // 2
        top = lax.broadcasted_iota(jnp.int32, (8, 256), 0) == 0
        for k in range(4):
            for d in range(16):
                kr[k, pl.ds(d, 1), :] = ks[k, pl.ds(0, 1), pl.ds(256 * d, 256)]

        @pl.when(me == n // 2)
        def _():
            row_copy().start()

        for k in range(4):
            for h in range(2):
                tiles = []
                for d in range(16):
                    tile = ks[k, pl.ds(8 * h, 8), pl.ds(256 * d, 256)]
                    if h == 0:
                        other = ks[k, pl.ds(16, 8), pl.ds(256 * d, 256)]
                        tile = jnp.where(jnp.logical_and(top, upper), other, tile)
                    tiles.append(tile)
                kt[k, h] = jnp.concatenate(tiles, 0).T

        @pl.when(me == n // 2)
        def _():
            row_copy().wait_send()

        @pl.when(me == 0)
        def _():
            row_copy().wait_recv()
            def both(k):
                return jnp.concatenate([kr[k], kr2[k]], 0)

            kst[0] = jnp.concatenate([both(0), both(1)] * 2, 0).T
            kst[1] = jnp.concatenate([both(3)] * 4, 0).T
            kst[2] = jnp.concatenate([both(2)] * 4, 0).T

    def step(it, _):
        def place(m, c):
            if isinstance(m, int) and m == 2:
                return 0, 16 * c
            return 1 + c // 8, pl.multiple_of(128 * m + 16 * (c % 8), 16)

        def y_first(m, _):
            @pl.when(it == 0)
            def _():
                arrived(m, fb.at[0], ty_recv)

            a = [fb[it, m, :, pl.ds(128 * k, 128)] for k in range(16)]
            real, imag = [None] * 17, [None] * 17
            for c in range(9):
                sums = []
                for odd in range(2):
                    re, im = None, None
                    for k in range(odd, 16, 2):
                        w = 2.0 * math.pi * (c * k % 32) / 32.0
                        wr, wi = round(math.cos(w), 15), round(-math.sin(w), 15)
                        if wr != 0.0:
                            re = a[k] * wr if re is None else re + a[k] * wr
                        if wi != 0.0:
                            im = a[k] * wi if im is None else im + a[k] * wi
                    zero = jnp.zeros_like(a[0])
                    sums.append((zero if re is None else re, zero if im is None else im))
                (er, ei), (ro, io) = sums
                real[c], imag[c] = er + ro, ei + io
                real[16 - c], imag[16 - c] = er - ro, io - ei
            for c in range(16):
                if c == 0:
                    vr, vi = real[0], real[16]
                else:
                    cos, sin = tw[pl.ds(512 + c, 1), :], tw[pl.ds(528 + c, 1), :]
                    vr, vi = real[c] * cos + imag[c] * sin, imag[c] * cos - real[c] * sin
                chunk, start = place(m, c)
                for part, v in enumerate((vr, vi)):
                    for k, piece in enumerate(split(v)):
                        u[k, chunk, pl.ds(start, 16), pl.ds(128 * part, 128)] = piece
            return 0

        def y_second(g, _):
            full = product(table(T_WA), (u[0, g], u[1, g]), LANES)
            first = product(table(T_WAQ), (u[0, g], u[1, g]), LANES)
            for part in range(2):
                for b in range(2):
                    block = (slice(128 * part, 128 * part + 128), slice(128 * b, 128 * b + 128))
                    inside = jnp.logical_and(lane < 16, g == 1 if b else g < 2)
                    s1[g, pl.ds(2 * part + b, 128, stride=4), :] = jnp.where(inside, first[block], full[block])
            exchange(g, s1, r1, a_send, a_recv)
            return 0

        @pl.when(it == 1)
        def _():
            sent(s1, a_send)
            sent(s2, b_send)

        y_first(2, 0)
        y_second(0, 0)
        lax.fori_loop(0, 2, y_first, 0)
        lax.fori_loop(1, 3, y_second, 0)

        halos = []
        for side, (to, row) in enumerate(((after, 15), (before, 0))):
            halos.append(pltpu.make_async_remote_copy(
                src_ref=fb.at[it, :, row], dst_ref=hb.at[it, side, pl.ds(0, 3)],
                send_sem=h_send.at[side], recv_sem=h_recv.at[it, side],
                device_id=(to // n_ty, lax.rem(to, n_ty)), device_id_type=MESH,
            ))
        for halo in halos:
            halo.start()

        @pl.when(it == 0)
        def _():
            kernel_tables()

        def mirrored_rows(g, group):
            dot = functools.partial(jnp.dot, preferred_element_type=F32)
            halves = lambda v: v[:, :128] + v[:, 128:]
            cos, sin = tw[pl.ds(0, 256), :], tw[pl.ds(256, 256), :]
            seq = jnp.zeros((128, 128), F32)
            for j in range(2):
                for b in range(len(group)):
                    block = r1[g, pl.ds(2 * j + b, 128, stride=4), :]
                    at = 32 * b + 16 * j
                    inside = jnp.logical_and(lane >= at, lane < at + 16)
                    seq = jnp.where(inside, pltpu.roll(block, at, 1) if at else block, seq)
            xh, xl = split(seq)
            x = jnp.concatenate([
                jnp.concatenate([xh, xl], 1), jnp.concatenate([jnp.zeros_like(xh), xh], 1)], 0)
            ar, ai = [
                halves(dot(jnp.concatenate([cb[0, k, :, pl.ds(0, 128)], cb[1, k, :, pl.ds(0, 128)]], 1), x))
                for k in (T_W1R, T_W1I)
            ]
            yield None
            vh, vl = split(jnp.concatenate([ar * cos + ai * sin, ai * cos - ar * sin], 1))
            z = halves(dot(vh, cb[0, T_SF])) + dot(vl, cb[0, T_SF, :, pl.ds(0, 128)])
            yield None
            wide = lax.broadcasted_iota(jnp.int32, (256, 128), 1)
            if len(group) == 1:
                field = kst[2] * z
            else:
                swapped = jnp.where(lax.rem(wide // 32, 2) == 0, pltpu.roll(z, 96, 1), pltpu.roll(z, 32, 1))
                field = kst[0] * z + kst[1] * swapped
            back = halves(dot(jnp.concatenate(split(field), 1), cb[0, T_SI]))
            yield None
            turned = pltpu.roll(back, 64, 1) * sin
            yh, yl = split(back * cos + jnp.where(wide < 64, -turned, turned))
            y = jnp.concatenate([yh, yl], 1)
            re, im = [
                halves(dot(cb[0, k, pl.ds(0, 128), :], y)) + dot(cb[1, k, pl.ds(0, 128), :], yh)
                for k in (T_BR, T_BI)
            ]
            yield re + pltpu.roll(im, 64, 1)

        def x_core(g, group, mirrored):
            aside = mirrored_rows(g, group) if mirrored else iter([None] * 4)
            for part in range(2):
                for b in range(2):
                    block = r1[g, pl.ds(2 * part + b, 128, stride=4), :]
                    for k, piece in enumerate(split(block)):
                        xs[k, pl.ds(128 * part, 128), pl.ds(128 * b, 128)] = piece
            x = (xs[0], xs[1])
            tr, ti = product(table(T_W1R), x), product(table(T_W1I), x)
            next(aside)
            cos, sin = tw[pl.ds(0, 256), :], tw[pl.ds(256, 256), :]
            for b in range(2):
                ar, ai = tr[:, 128 * b:128 * b + 128], ti[:, 128 * b:128 * b + 128]
                v = jnp.concatenate([ar * cos + ai * sin, ai * cos - ar * sin], 1)
                zb[b] = product(split(v), table(T_W2))

            next(aside)
            for b in range(2):
                pieces = []
                for part in range(2):
                    cols = pl.ds(128 * part, 128)
                    if len(group) == 1:
                        pieces.append(kt[2, b] * zb[b, :, cols])
                    else:
                        pieces.append(kt[b, g - 1] * zb[b, :, cols] + kt[3, g - 1] * zb[1 - b, :, cols])
                p = product(split(jnp.concatenate(pieces, 1)), table(T_W2I))
                if b == 0:
                    next(aside)
                pr, pi = p[:, :128], p[:, 128:]
                for part, v in enumerate((pr * cos - pi * sin, pi * cos + pr * sin)):
                    for k, piece in enumerate(split(v)):
                        ys[k, part, :, pl.ds(128 * b, 128)] = piece
            moved = next(aside)
            o = product(table(T_BR), (ys[0, 0], ys[1, 0])) + product(table(T_BI), (ys[0, 1], ys[1, 1]))
            for part in range(2):
                for b in range(2):
                    s2[g, pl.ds(2 * part + b, 128, stride=4), :] = (
                        o[128 * part:128 * part + 128, 128 * b:128 * b + 128])

            if mirrored:
                for j in range(2):
                    for b in range(len(group)):
                        rows = pl.ds(2 * j + b, 128, stride=4)
                        shift = (128 - 32 * b - 16 * j) % 128
                        own_lanes = pltpu.roll(moved, shift, 1) if shift else moved
                        block = o[128 * j:128 * j + 128, 128 * b:128 * b + 128]
                        s2[g, rows, :] = jnp.where(lane < 16, own_lanes, block)

        def x_chunk(g, group):
            arrived(g, r1, a_recv)
            mirrored = me == 0 if len(group) == 1 else jnp.logical_and(me == 0, g == 1)
            pl.when(mirrored)(lambda: x_core(g, group, True))
            pl.when(jnp.logical_not(mirrored))(lambda: x_core(g, group, False))
            exchange(g, s2, r2, b_send, b_recv)

        def xy_chunk(g, _):
            x_chunk(g, (0, 1))
            return 0

        x_chunk(0, (2,))
        lax.fori_loop(1, 3, xy_chunk, 0)

        for halo in halos:
            halo.wait_recv()
        row = lax.broadcasted_iota(jnp.int32, (16, 2048), 0)
        col = lax.broadcasted_iota(jnp.int32, (16, 2048), 1)
        for m in range(3):
            f = fb[it, m]
            low = jnp.where(me > 0, hb[it, 0, pl.ds(m, 1), :], 0.0)
            high = jnp.where(me < n - 1, hb[it, 1, pl.ds(m, 1), :], 0.0)
            up = jnp.where(row == 0, low, pltpu.roll(f, 1, 0))
            down = jnp.where(row == 15, high, pltpu.roll(f, 15, 0))
            left = jnp.where(col == 0, 0.0, pltpu.roll(f, 1, 1))
            right = jnp.where(col == 2047, 0.0, pltpu.roll(f, 2047, 1))
            ex[m] = STIFFNESS * (down + up + right + left)
        for halo in halos:
            halo.wait_send()

        def y_inverse_first(g, _):
            arrived(g, r2, b_recv)
            for part in range(2):
                for b in range(2):
                    block = r2[g, pl.ds(2 * part + b, 128, stride=4), :].T
                    for k, piece in enumerate(split(block)):
                        xs[k, pl.ds(128 * b, 128), pl.ds(128 * part, 128)] = piece
            pb[g] = product((xs[0], xs[1]), table(T_W3))

            def ends(m, row):
                rows = pl.ds(row, 16)
                pq[m] = product((xs[0, rows, :], xs[1, rows, :]), table(T_W3Q))

            if isinstance(g, int):
                ends(2, 0)
            else:
                @pl.when(g == 1)
                def _():
                    ends(0, 0)
                    ends(1, 128)

            return 0

        def y_inverse_second(m, _):
            real, imag = [None] * 16, [None] * 16
            for c in range(1, 16):
                cos, sin = tw[pl.ds(512 + c, 1), :], tw[pl.ds(528 + c, 1), :]
                chunk, start = place(m, c)
                br, bi = pb[chunk, pl.ds(start, 16), pl.ds(0, 128)], pb[chunk, pl.ds(start, 16), pl.ds(128, 128)]
                real[c], imag[c] = br * cos - bi * sin, bi * cos + br * sin
            even, odd_part = pq[m, :, pl.ds(0, 128)], pq[m, :, pl.ds(128, 128)]
            ends = (even + odd_part, even - odd_part)
            pairs = []
            for odd in range(2):
                pairs.append([
                    (real[c] - real[16 - c], imag[c] + imag[16 - c]) if odd
                    else (real[c] + real[16 - c], imag[c] - imag[16 - c]) for c in range(1, 8)
                ])
            for a in range(16):
                total = ends[a % 2]
                for c in range(1, 9):
                    re, im = pairs[a % 2][c - 1] if c < 8 else (real[8], imag[8])
                    w = 2.0 * math.pi * (c * a % 32) / 32.0
                    wr, wi = round(math.cos(w), 15), round(math.sin(w), 15)
                    if wr != 0.0:
                        total = total + re * wr
                    if wi != 0.0:
                        total = total - im * wi
                dm[m, :, pl.ds(128 * a, 128)] = total
            return 0

        y_inverse_first(0, 0)
        y_inverse_second(2, 0)
        lax.fori_loop(1, 3, y_inverse_first, 0)
        lax.fori_loop(0, 2, y_inverse_second, 0)

        def advance(j, _):
            far = j // 2
            dz = jnp.where(far == 0, 2, jnp.where(far == 1, 1, jnp.where(far == 2, 3, 0)))
            to = lax.rem(pz + dz, n_z) * 2 + lax.rem(pc + j + 1, 2)
            cols = pl.ds(pl.multiple_of(to * 256, 256), 256)
            m0 = [fb[0, m, :, cols] for m in range(3)]
            f = [fb[it, m, :, cols] for m in range(3)]
            heff = [dm[m, :, cols] + ex[m, :, cols] for m in range(3)]
            torque = cross(f, heff)
            damped = cross(f, torque)
            rate = [(t + DAMPING * d) * (-1.0 / (1.0 + DAMPING * DAMPING)) for t, d in zip(torque, damped)]

            @pl.when(it == 0)
            def _():
                filled = jnp.where(squared(m0) > 0.5, 0.0, 1.0)
                v = [m + TIME_STEP * r for m, r in zip(m0, rate)]
                root = jnp.sqrt(squared(v) + filled)
                for m in range(3):
                    k1[m, :, cols] = rate[m]
                    fb[1, m, :, cols] = v[m] / root

            @pl.when(it == 1)
            def _():
                along = rate[0] * m0[0] + rate[1] * m0[1] + rate[2] * m0[2]
                for m in range(3):
                    mr[m, :, cols] = k1[m, :, cols] + (rate[m] - along * m0[m])

                @pl.when(j < n_ty - 1)
                def _():
                    pltpu.make_async_remote_copy(
                        src_ref=mr.at[:, :, cols], dst_ref=out_ref.at[:, own_rows, :],
                        send_sem=f_send, recv_sem=f_recv, device_id=(tx, to), device_id_type=MESH,
                    ).start()

                @pl.when(j == n_ty - 1)
                def _():
                    pltpu.make_async_copy(mr.at[:, :, cols], out_ref.at[:, own_rows, :], f_recv).start()

            return 0

        lax.fori_loop(0, n_ty, advance, 0)
        return 0

    lax.fori_loop(0, 2, step, 0)
    rest = m0l.at[:, pl.ds(0, 16 * (n_ty - 1)), :]
    pltpu.make_async_copy(rest, rest, ty_send).wait()
    sent(s1, a_send)
    sent(s2, b_send)
    pltpu.make_async_copy(out_ref, out_ref, f_recv).wait()
    pltpu.make_async_copy(rest, rest, f_send).wait()


def body(sizes, mag, occupancy, kernel_spectrum):
    cb = jnp.asarray(two_parts(matrices()))
    tw = jnp.asarray(twiddles())
    V = pltpu.VMEM
    D = pltpu.SemaphoreType.DMA
    block = (3, 128, 256)
    band = (3, 16, 2048)
    slots = (3, 512, 128)
    doubled = pl.pallas_call(
        functools.partial(kernel, sizes),
        out_shape=jax.ShapeDtypeStruct(block, F32),
        in_specs=[pl.BlockSpec(memory_space=pl.ANY)] * 5,
        out_specs=pl.BlockSpec(memory_space=pltpu.VMEM),
        scratch_shapes=[
            V(block, F32), V((128, 256), jnp.int32), V((4, 24, 4096), F32), V((2, N_TABLES, 256, 256), BF16),
            V((544, 128), F32),
            V(block, F32), V((2,) + band, F32), V(band, F32), V(band, F32), V(band, F32),
            V(band, F32), V((2, 2, 8, 2048), F32), V((4, 2, 256, 128), F32),
            V((4, 16, 256), F32), V((4, 16, 256), F32), V((3, 256, 128), F32),
            V(slots, F32), V(slots, F32), V(slots, F32), V(slots, F32),
            V((2, 3, 256, 256), BF16), V((2, 256, 256), F32), V((2, 256, 256), BF16), V((2, 2, 256, 256), BF16),
            V((3, 256, 256), F32), V((3, 16, 256), F32),
            D((5,)), D, D((3,)), D((2,)), D((2, 2)), D, D, D, D((3,)), D, D((3,)), D, D,
            pltpu.SemaphoreType.REGULAR,
        ],
        compiler_params=pltpu.CompilerParams(
            collective_id=0, has_side_effects=True, vmem_limit_bytes=56 * 1024 * 1024
        ),
    )(mag, occupancy, kernel_spectrum, cb, tw)
    late, doubled = lax.optimization_barrier((occupancy, doubled))
    occ = late.astype(F32)
    mean_rate = 0.5 * doubled
    v = [mag[m] * occ + TIME_STEP * mean_rate[m] for m in range(3)]
    root = jnp.sqrt(squared(v) + 1.0 - occ)
    return jnp.stack([c / root for c in v]), mean_rate


def solution(mesh):
    n_tx, n_ty = mesh.shape["tx"], mesh.shape["ty"]
    side = math.isqrt(n_tx)
    return jax.shard_map(
        functools.partial(body, (side, side, n_ty // 2)),
        mesh=mesh,
        in_specs=(P(None, "tx", "ty"), P("tx", "ty"), P(None, ("tx", "ty"), None)),
        out_specs=(P(None, "tx", "ty"), P(None, "tx", "ty")),
        check_vma=False,
    )
```

```python
import functools
import itertools
import math

import jax
import jax.numpy as jnp
import ml_dtypes
import numpy as np
from jax import lax
from jax.experimental import pallas as pl
from jax.experimental.pallas import tpu as pltpu
from jax.sharding import PartitionSpec as P

DAMPING = 0.3
STIFFNESS = 0.25
TIME_STEP = 0.25
MESH = pl.DeviceIdType.MESH
F32 = jnp.float32
BF16 = jnp.bfloat16


(T_WA, T_WAQ, T_W1R, T_W1I, T_W2, T_W2I, T_BR, T_BI, T_W3, T_W3Q, T_SF, T_SI) = range(12)
N_TABLES = 12


def angle(left, right, length):
    product = np.arange(left)[:, None] * np.arange(right)[None, :] % length
    return 2.0 * math.pi * product / length


def matrices():
    out = np.zeros((N_TABLES, 256, 256))
    th = angle(128, 128, 128)
    cos, sin = np.cos(th), np.sin(th)
    out[T_WA] = np.block([[cos, sin], [-sin, cos]])
    scale = -(2.0**-24)
    out[T_W3] = 2.0 * scale * np.block([[cos, sin], [-sin, cos]])
    ph = th + 2.0 * math.pi * np.arange(128)[None, :] / 256.0
    low, high = np.arange(1, 64), np.arange(64, 128)
    sign = 1.0 - 2.0 * (np.arange(128) % 2)
    q = np.zeros((2, 128, 2, 128))
    q[0, 0, 0], q[1, 0, 0] = 1.0, sign
    q[0, low, 0], q[1, low, 0] = cos[low], -sin[low]
    q[0, high, 1], q[1, high, 1] = np.cos(ph)[high], -np.sin(ph)[high]
    out[T_WAQ] = q.reshape(256, 256)
    weight = np.full((128, 1, 1), 2.0)
    weight[0] = 1.0
    out[T_W3Q] = scale * (q * weight).reshape(256, 256)
    th = angle(256, 128, 256)
    cos, sin = np.cos(th), np.sin(th)
    out[T_W1R] = np.concatenate([cos, sin], 1)
    out[T_W1I] = np.concatenate([-sin, cos], 1)
    out[T_BR] = np.concatenate([cos.T, sin.T], 0)
    out[T_BI] = np.concatenate([-sin.T, cos.T], 0)
    th = angle(16, 16, 16)
    cos, sin = np.cos(th), np.sin(th)
    eight = np.eye(8)
    wc = np.einsum("ab,id->aidb", eight, cos).reshape(128, 128)
    ws = np.einsum("ab,id->aidb", eight, sin).reshape(128, 128)
    out[T_W2] = np.block([[wc, -ws], [ws, wc]])
    out[T_W2I] = np.block([[wc.T, ws.T], [-ws.T, wc.T]])
    four = np.eye(4)
    sc = np.kron(four, cos)
    ss = np.kron(four, sin)
    none = np.zeros((64, 64))
    out[T_SF, :, :128] = np.block([[sc, -ss], [none, none], [ss, sc], [none, none]])
    out[T_SI, :128, :128] = np.block([[sc.T, ss.T], [-ss.T, sc.T]])
    return out


def two_parts(value):
    high = value.astype(np.float32).astype(ml_dtypes.bfloat16)
    low = (value - high.astype(np.float64)).astype(np.float32).astype(ml_dtypes.bfloat16)
    both = np.stack([high, low])
    for k in (T_SF, T_SI):
        both[0, k, :, 128:] = low[k, :, :128]
    both[0, T_SI, 128:, :128] = high[T_SI, :128, :128]
    return both


def twiddles():
    th = 2.0 * math.pi * (np.arange(256)[:, None] * (np.arange(128) % 16)[None, :]) / 4096.0
    ty = angle(16, 128, 4096)
    return np.concatenate([np.cos(th), np.sin(th), np.cos(ty), np.sin(ty)], 0).astype(np.float32)


def split(value):
    high = value.astype(BF16)
    return high, (value - high.astype(F32)).astype(BF16)


def product(a, b, form=(((1,), (0,)), ((), ()))):
    dot = functools.partial(lax.dot_general, dimension_numbers=form, preferred_element_type=F32)
    return dot(a[0], b[0]) + (dot(a[0], b[1]) + dot(a[1], b[0]))


LANES = (((1,), (1,)), ((), ()))


def cross(left, right):
    return [
        left[1] * right[2] - left[2] * right[1],
        left[2] * right[0] - left[0] * right[2],
        left[0] * right[1] - left[1] * right[0],
    ]


def squared(v):
    return v[0] * v[0] + v[1] * v[1] + v[2] * v[2]


def far_first(n_x, n_y, n_z):
    def far(o):
        return sum(min(d, k - d) for d, k in zip(o, (n_x, n_y, n_z)))

    offsets = [o for o in itertools.product(range(n_x), range(n_y), range(n_z), range(2)) if any(o)]
    mixed = np.random.RandomState(1).permutation(len(offsets))
    return sorted((offsets[k] for k in mixed), key=lambda o: -far(o))


def kernel(sizes, mag_h, occ_h, ks_h, cb_h, tw_h, out_ref, mag, occ, ks, cb, tw, m0l, fb, k1, dm, ex,
           mr, hb, kt, kr, kr2, kst, s1, r1, s2, r2, u, xs, ys, pb, pq, load_sem, ty_send, ty_recv,
           h_send, h_recv, k_send, k_recv, a_send, a_recv, b_send, b_recv, f_send, f_recv, ready):
    n_x, n_y, n_z = sizes
    n_ty = 2 * n_z
    n = n_x * n_y * n_ty
    tx, ty = lax.axis_index("tx"), lax.axis_index("ty")
    me = tx * n_ty + ty
    px, py, pz, pc = tx // n_y, lax.rem(tx, n_y), ty // 2, lax.rem(ty, 2)
    at_x = [lax.rem(px + d, n_x) * n_y for d in range(n_x)]
    at_y = [lax.rem(py + d, n_y) for d in range(n_y)]
    at_z = [lax.rem(pz + d, n_z) * 2 for d in range(n_z)]
    at_c = [pc, 1 - pc]
    others = far_first(n_x, n_y, n_z)

    barrier = pltpu.get_barrier_semaphore()
    line = [o for o in others if o[:2] == (0, 0)]
    plane = [o for o in others if o[2:] == (0, 0)]
    for dx, dy, dz, dc in plane + line:
        to = (at_x[dx] + at_y[dy], at_z[dz] + at_c[dc])
        pl.semaphore_signal(barrier, inc=1, device_id=to, device_id_type=MESH)

    loads = [
        pltpu.make_async_copy(mag_h, mag, load_sem.at[0]),
        pltpu.make_async_copy(occ_h, occ, load_sem.at[1]),
        pltpu.make_async_copy(ks_h.at[:, pl.ds(0, 24), :], ks, load_sem.at[2]),
        pltpu.make_async_copy(cb_h, cb, load_sem.at[3]),
        pltpu.make_async_copy(tw_h, tw, load_sem.at[4]),
    ]
    for k in (0, 1, 4, 3, 2):
        loads[k].start()
    loads[0].wait()
    loads[1].wait()
    occf = occ[...].astype(F32)
    for m in range(3):
        m0l[m] = mag[m] * occf
    pl.semaphore_wait(barrier, len(plane) + len(line))

    def table(k):
        return cb[0, k], cb[1, k]

    mine = pl.ds(pl.multiple_of(ty * 256, 256), 256)
    own_rows = pl.ds(pl.multiple_of(ty * 16, 16), 16)
    for m in (2, 0, 1):
        for _, _, dz, dc in line:
            to = at_z[dz] + at_c[dc]
            pltpu.make_async_remote_copy(
                src_ref=m0l.at[m, pl.ds(pl.multiple_of(to * 16, 16), 16), :], dst_ref=fb.at[0, m, :, mine],
                send_sem=ty_send, recv_sem=ty_recv.at[m], device_id=(tx, to), device_id_type=MESH,
            ).start()
        pltpu.make_async_copy(m0l.at[m, own_rows, :], fb.at[0, m, :, mine], ty_recv.at[m]).start()

    for _, _, dz, dc in line:
        pl.semaphore_signal(ready, inc=1, device_id=(tx, at_z[dz] + at_c[dc]), device_id_type=MESH)
    loads[3].wait()
    loads[4].wait()
    pl.semaphore_wait(ready, len(line))
    own = pl.ds(pl.multiple_of(me * 4, 4), 4)

    def exchange(m, source, target, send, recv):
        for dx, dy, dz, dc in others:
            a, b = at_x[dx] + at_y[dy], at_z[dz] + at_c[dc]
            there = pl.ds(pl.multiple_of((a * n_ty + b) * 4, 4), 4)
            pltpu.make_async_remote_copy(
                src_ref=source.at[m, there, :], dst_ref=target.at[m, own, :],
                send_sem=send, recv_sem=recv.at[m], device_id=(a, b), device_id_type=MESH,
            ).start()
        pltpu.make_async_copy(source.at[m, own, :], target.at[m, own, :], recv.at[m]).start()

    def arrived(m, target, recv):
        pltpu.make_async_copy(target.at[m], target.at[m], recv.at[m]).wait()

    def sent(source, send):
        rest = source.at[:, pl.ds(0, 4 * (n - 1)), :]
        pltpu.make_async_copy(rest, rest, send).wait()

    lane = lax.broadcasted_iota(jnp.int32, (128, 128), 1)
    after, before = lax.rem(me + 1, n), lax.rem(me + n - 1, n)

    def row_copy():
        return pltpu.make_async_remote_copy(
            src_ref=kr, dst_ref=kr2, send_sem=k_send, recv_sem=k_recv, device_id=(0, 0), device_id_type=MESH
        )

    def kernel_tables():
        loads[2].wait()
        upper = me >= n // 2
        top = lax.broadcasted_iota(jnp.int32, (8, 256), 0) == 0
        for k in range(4):
            for d in range(16):
                kr[k, pl.ds(d, 1), :] = ks[k, pl.ds(0, 1), pl.ds(256 * d, 256)]

        @pl.when(me == n // 2)
        def _():
            row_copy().start()

        for k in range(4):
            for h in range(2):
                tiles = []
                for d in range(16):
                    tile = ks[k, pl.ds(8 * h, 8), pl.ds(256 * d, 256)]
                    if h == 0:
                        other = ks[k, pl.ds(16, 8), pl.ds(256 * d, 256)]
                        tile = jnp.where(jnp.logical_and(top, upper), other, tile)
                    tiles.append(tile)
                kt[k, h] = jnp.concatenate(tiles, 0).T

        @pl.when(me == n // 2)
        def _():
            row_copy().wait_send()

        @pl.when(me == 0)
        def _():
            row_copy().wait_recv()
            def both(k):
                return jnp.concatenate([kr[k], kr2[k]], 0)

            kst[0] = jnp.concatenate([both(0), both(1)] * 2, 0).T
            kst[1] = jnp.concatenate([both(3)] * 4, 0).T
            kst[2] = jnp.concatenate([both(2)] * 4, 0).T

    def step(it, _):
        def place(m, c):
            if isinstance(m, int) and m == 2:
                return 0, 16 * c
            start = 128 * m + 16 * (c % 8)
            return 1 + c // 8, start if isinstance(m, int) else pl.multiple_of(start, 16)

        def y_first(m, _):
            @pl.when(it == 0)
            def _():
                arrived(m, fb.at[0], ty_recv)

            a = [fb[it, m, :, pl.ds(128 * k, 128)] for k in range(16)]
            real, imag = [None] * 17, [None] * 17
            for c in range(9):
                sums = []
                for odd in range(2):
                    re, im = None, None
                    for k in range(odd, 16, 2):
                        w = 2.0 * math.pi * (c * k % 32) / 32.0
                        wr, wi = round(math.cos(w), 15), round(-math.sin(w), 15)
                        if wr != 0.0:
                            re = a[k] * wr if re is None else re + a[k] * wr
                        if wi != 0.0:
                            im = a[k] * wi if im is None else im + a[k] * wi
                    zero = jnp.zeros_like(a[0])
                    sums.append((zero if re is None else re, zero if im is None else im))
                (er, ei), (ro, io) = sums
                real[c], imag[c] = er + ro, ei + io
                real[16 - c], imag[16 - c] = er - ro, io - ei
            for c in range(16):
                if c == 0:
                    vr, vi = real[0], real[16]
                else:
                    cos, sin = tw[pl.ds(512 + c, 1), :], tw[pl.ds(528 + c, 1), :]
                    vr, vi = real[c] * cos + imag[c] * sin, imag[c] * cos - real[c] * sin
                chunk, start = place(m, c)
                for part, v in enumerate((vr, vi)):
                    for k, piece in enumerate(split(v)):
                        u[k, chunk, pl.ds(start, 16), pl.ds(128 * part, 128)] = piece
            return 0

        def y_second(g, _):
            full = product(table(T_WA), (u[0, g], u[1, g]), LANES)
            first = product(table(T_WAQ), (u[0, g], u[1, g]), LANES)
            for part in range(2):
                for b in range(2):
                    block = (slice(128 * part, 128 * part + 128), slice(128 * b, 128 * b + 128))
                    inside = jnp.logical_and(lane < 16, g == 1 if b else g < 2)
                    s1[g, pl.ds(2 * part + b, 128, stride=4), :] = jnp.where(inside, first[block], full[block])
            exchange(g, s1, r1, a_send, a_recv)
            return 0

        @pl.when(it == 1)
        def _():
            sent(s1, a_send)
            sent(s2, b_send)

        y_first(2, 0)
        y_second(0, 0)
        lax.fori_loop(0, 2, y_first, 0)
        lax.fori_loop(1, 3, y_second, 0)

        halos = []
        for side, (to, row) in enumerate(((after, 15), (before, 0))):
            halos.append(pltpu.make_async_remote_copy(
                src_ref=fb.at[it, :, row], dst_ref=hb.at[it, side, pl.ds(0, 3)],
                send_sem=h_send.at[side], recv_sem=h_recv.at[it, side],
                device_id=(to // n_ty, lax.rem(to, n_ty)), device_id_type=MESH,
            ))
        for halo in halos:
            halo.start()

        @pl.when(it == 0)
        def _():
            kernel_tables()

        def mirrored_rows(g, group):
            dot = functools.partial(jnp.dot, preferred_element_type=F32)
            halves = lambda v: v[:, :128] + v[:, 128:]
            cos, sin = tw[pl.ds(0, 256), :], tw[pl.ds(256, 256), :]
            seq = jnp.zeros((128, 128), F32)
            for j in range(2):
                for b in range(len(group)):
                    block = r1[g, pl.ds(2 * j + b, 128, stride=4), :]
                    at = 32 * b + 16 * j
                    inside = jnp.logical_and(lane >= at, lane < at + 16)
                    seq = jnp.where(inside, pltpu.roll(block, at, 1) if at else block, seq)
            xh, xl = split(seq)
            x = jnp.concatenate([
                jnp.concatenate([xh, xl], 1), jnp.concatenate([jnp.zeros_like(xh), xh], 1)], 0)
            ar, ai = [
                halves(dot(jnp.concatenate([cb[0, k, :, pl.ds(0, 128)], cb[1, k, :, pl.ds(0, 128)]], 1), x))
                for k in (T_W1R, T_W1I)
            ]
            yield None
            vh, vl = split(jnp.concatenate([ar * cos + ai * sin, ai * cos - ar * sin], 1))
            z = halves(dot(vh, cb[0, T_SF])) + dot(vl, cb[0, T_SF, :, pl.ds(0, 128)])
            yield None
            wide = lax.broadcasted_iota(jnp.int32, (256, 128), 1)
            if len(group) == 1:
                field = kst[2] * z
            else:
                swapped = jnp.where(lax.rem(wide // 32, 2) == 0, pltpu.roll(z, 96, 1), pltpu.roll(z, 32, 1))
                field = kst[0] * z + kst[1] * swapped
            back = halves(dot(jnp.concatenate(split(field), 1), cb[0, T_SI]))
            yield None
            turned = pltpu.roll(back, 64, 1) * sin
            yh, yl = split(back * cos + jnp.where(wide < 64, -turned, turned))
            y = jnp.concatenate([yh, yl], 1)
            re, im = [
                halves(dot(cb[0, k, pl.ds(0, 128), :], y)) + dot(cb[1, k, pl.ds(0, 128), :], yh)
                for k in (T_BR, T_BI)
            ]
            yield re + pltpu.roll(im, 64, 1)

        def x_core(g, group, mirrored):
            aside = mirrored_rows(g, group) if mirrored else iter([None] * 4)
            x = split(jnp.concatenate([
                jnp.concatenate([r1[g, pl.ds(2 * part + b, 128, stride=4), :] for b in range(2)], 1)
                for part in range(2)], 0))
            tr, ti = product(table(T_W1R), x), product(table(T_W1I), x)
            next(aside)
            cos, sin = tw[pl.ds(0, 256), :], tw[pl.ds(256, 256), :]
            zs = []
            for b in range(2):
                ar, ai = tr[:, 128 * b:128 * b + 128], ti[:, 128 * b:128 * b + 128]
                v = jnp.concatenate([ar * cos + ai * sin, ai * cos - ar * sin], 1)
                zs.append(product(split(v), table(T_W2)))

            next(aside)
            for b in range(2):
                pieces = []
                for part in range(2):
                    cols = slice(128 * part, 128 * part + 128)
                    if len(group) == 1:
                        pieces.append(kt[2, b] * zs[b][:, cols])
                    else:
                        pieces.append(kt[b, g - 1] * zs[b][:, cols] + kt[3, g - 1] * zs[1 - b][:, cols])
                p = product(split(jnp.concatenate(pieces, 1)), table(T_W2I))
                if b == 0:
                    next(aside)
                pr, pi = p[:, :128], p[:, 128:]
                for part, v in enumerate((pr * cos - pi * sin, pi * cos + pr * sin)):
                    for k, piece in enumerate(split(v)):
                        ys[k, part, :, pl.ds(128 * b, 128)] = piece
            moved = next(aside)
            o = product(table(T_BR), (ys[0, 0], ys[1, 0])) + product(table(T_BI), (ys[0, 1], ys[1, 1]))
            for part in range(2):
                for b in range(2):
                    s2[g, pl.ds(2 * part + b, 128, stride=4), :] = (
                        o[128 * part:128 * part + 128, 128 * b:128 * b + 128])

            if mirrored:
                for j in range(2):
                    for b in range(len(group)):
                        rows = pl.ds(2 * j + b, 128, stride=4)
                        shift = (128 - 32 * b - 16 * j) % 128
                        own_lanes = pltpu.roll(moved, shift, 1) if shift else moved
                        block = o[128 * j:128 * j + 128, 128 * b:128 * b + 128]
                        s2[g, rows, :] = jnp.where(lane < 16, own_lanes, block)

        def x_chunk(g, group):
            arrived(g, r1, a_recv)
            mirrored = me == 0 if len(group) == 1 else jnp.logical_and(me == 0, g == 1)
            pl.when(mirrored)(lambda: x_core(g, group, True))
            pl.when(jnp.logical_not(mirrored))(lambda: x_core(g, group, False))
            exchange(g, s2, r2, b_send, b_recv)

        def xy_chunk(g, _):
            x_chunk(g, (0, 1))
            return 0

        x_chunk(0, (2,))
        lax.fori_loop(1, 3, xy_chunk, 0)

        for halo in halos:
            halo.wait_recv()
        row = lax.broadcasted_iota(jnp.int32, (16, 2048), 0)
        col = lax.broadcasted_iota(jnp.int32, (16, 2048), 1)
        for m in range(3):
            f = fb[it, m]
            low = jnp.where(me > 0, hb[it, 0, pl.ds(m, 1), :], 0.0)
            high = jnp.where(me < n - 1, hb[it, 1, pl.ds(m, 1), :], 0.0)
            up = jnp.where(row == 0, low, pltpu.roll(f, 1, 0))
            down = jnp.where(row == 15, high, pltpu.roll(f, 15, 0))
            left = jnp.where(col == 0, 0.0, pltpu.roll(f, 1, 1))
            right = jnp.where(col == 2047, 0.0, pltpu.roll(f, 2047, 1))
            ex[m] = STIFFNESS * (down + up + right + left)
        for halo in halos:
            halo.wait_send()

        def y_inverse_first(g, _):
            arrived(g, r2, b_recv)
            for part in range(2):
                for b in range(2):
                    block = r2[g, pl.ds(2 * part + b, 128, stride=4), :]
                    for k, piece in enumerate(split(block)):
                        xs[k, pl.ds(128 * part, 128), pl.ds(128 * b, 128)] = piece
            rows_first = (((0,), (0,)), ((), ()))
            pb[g] = product((xs[0], xs[1]), table(T_W3), rows_first)

            def ends(m, row):
                cols = pl.ds(row, 128)
                pq[m] = product((xs[0, :, cols], xs[1, :, cols]), table(T_W3Q), rows_first)[:16]

            if isinstance(g, int):
                ends(2, 0)
            else:
                @pl.when(g == 1)
                def _():
                    ends(0, 0)
                    ends(1, 128)

            return 0

        def y_inverse_second(m, _):
            real, imag = [None] * 16, [None] * 16
            for c in range(1, 16):
                cos, sin = tw[pl.ds(512 + c, 1), :], tw[pl.ds(528 + c, 1), :]
                chunk, start = place(m, c)
                br, bi = pb[chunk, pl.ds(start, 16), pl.ds(0, 128)], pb[chunk, pl.ds(start, 16), pl.ds(128, 128)]
                real[c], imag[c] = br * cos - bi * sin, bi * cos + br * sin
            even, odd_part = pq[m, :, pl.ds(0, 128)], pq[m, :, pl.ds(128, 128)]
            ends = (even + odd_part, even - odd_part)
            pairs = []
            for odd in range(2):
                pairs.append([
                    (real[c] - real[16 - c], imag[c] + imag[16 - c]) if odd
                    else (real[c] + real[16 - c], imag[c] - imag[16 - c]) for c in range(1, 8)
                ])
            for a in range(16):
                total = ends[a % 2]
                for c in range(1, 9):
                    re, im = pairs[a % 2][c - 1] if c < 8 else (real[8], imag[8])
                    w = 2.0 * math.pi * (c * a % 32) / 32.0
                    wr, wi = round(math.cos(w), 15), round(math.sin(w), 15)
                    if wr != 0.0:
                        total = total + re * wr
                    if wi != 0.0:
                        total = total - im * wi
                dm[m, :, pl.ds(128 * a, 128)] = total
            return 0

        y_inverse_first(0, 0)
        y_inverse_second(2, 0)
        lax.fori_loop(1, 3, y_inverse_first, 0)
        y_inverse_second(0, 0)
        y_inverse_second(1, 0)

        def advance(j, _):
            far = j // 2
            dz = jnp.where(far == 0, 2, jnp.where(far == 1, 1, jnp.where(far == 2, 3, 0)))
            to = lax.rem(pz + dz, n_z) * 2 + lax.rem(pc + j + 1, 2)
            cols = pl.ds(pl.multiple_of(to * 256, 256), 256)
            m0 = [fb[0, m, :, cols] for m in range(3)]
            f = [fb[it, m, :, cols] for m in range(3)]
            heff = [dm[m, :, cols] + ex[m, :, cols] for m in range(3)]
            torque = cross(f, heff)
            damped = cross(f, torque)
            rate = [(t + DAMPING * d) * (-1.0 / (1.0 + DAMPING * DAMPING)) for t, d in zip(torque, damped)]

            @pl.when(it == 0)
            def _():
                filled = jnp.where(squared(m0) > 0.5, 0.0, 1.0)
                v = [m + TIME_STEP * r for m, r in zip(m0, rate)]
                root = jnp.sqrt(squared(v) + filled)
                for m in range(3):
                    k1[m, :, cols] = rate[m]
                    fb[1, m, :, cols] = v[m] / root

            @pl.when(it == 1)
            def _():
                along = rate[0] * m0[0] + rate[1] * m0[1] + rate[2] * m0[2]
                for m in range(3):
                    mr[m, :, cols] = k1[m, :, cols] + (rate[m] - along * m0[m])

                @pl.when(j < n_ty - 1)
                def _():
                    pltpu.make_async_remote_copy(
                        src_ref=mr.at[:, :, cols], dst_ref=out_ref.at[:, own_rows, :],
                        send_sem=f_send, recv_sem=f_recv, device_id=(tx, to), device_id_type=MESH,
                    ).start()

                @pl.when(j == n_ty - 1)
                def _():
                    pltpu.make_async_copy(mr.at[:, :, cols], out_ref.at[:, own_rows, :], f_recv).start()

            return 0

        lax.fori_loop(0, n_ty, advance, 0)
        return 0

    lax.fori_loop(0, 2, step, 0)
    rest = m0l.at[:, pl.ds(0, 16 * (n_ty - 1)), :]
    pltpu.make_async_copy(rest, rest, ty_send).wait()
    sent(s1, a_send)
    sent(s2, b_send)
    pltpu.make_async_copy(out_ref, out_ref, f_recv).wait()
    pltpu.make_async_copy(rest, rest, f_send).wait()


def body(sizes, mag, occupancy, kernel_spectrum):
    cb = jnp.asarray(two_parts(matrices()))
    tw = jnp.asarray(twiddles())
    V = pltpu.VMEM
    D = pltpu.SemaphoreType.DMA
    block = (3, 128, 256)
    band = (3, 16, 2048)
    slots = (3, 512, 128)
    doubled = pl.pallas_call(
        functools.partial(kernel, sizes),
        out_shape=jax.ShapeDtypeStruct(block, F32),
        in_specs=[pl.BlockSpec(memory_space=pl.ANY)] * 5,
        out_specs=pl.BlockSpec(memory_space=pltpu.VMEM),
        scratch_shapes=[
            V(block, F32), V((128, 256), jnp.int32), V((4, 24, 4096), F32), V((2, N_TABLES, 256, 256), BF16),
            V((544, 128), F32),
            V(block, F32), V((2,) + band, F32), V(band, F32), V(band, F32), V(band, F32),
            V(band, F32), V((2, 2, 8, 2048), F32), V((4, 2, 256, 128), F32),
            V((4, 16, 256), F32), V((4, 16, 256), F32), V((3, 256, 128), F32),
            V(slots, F32), V(slots, F32), V(slots, F32), V(slots, F32),
            V((2, 3, 256, 256), BF16), V((2, 256, 256), BF16), V((2, 2, 256, 256), BF16),
            V((3, 256, 256), F32), V((3, 16, 256), F32),
            D((5,)), D, D((3,)), D((2,)), D((2, 2)), D, D, D, D((3,)), D, D((3,)), D, D,
            pltpu.SemaphoreType.REGULAR,
        ],
        compiler_params=pltpu.CompilerParams(
            collective_id=0, has_side_effects=True, vmem_limit_bytes=56 * 1024 * 1024
        ),
    )(mag, occupancy, kernel_spectrum, cb, tw)
    late, doubled = lax.optimization_barrier((occupancy, doubled))
    occ = late.astype(F32)
    mean_rate = 0.5 * doubled
    v = [mag[m] * occ + TIME_STEP * mean_rate[m] for m in range(3)]
    root = jnp.sqrt(squared(v) + 1.0 - occ)
    return jnp.stack([c / root for c in v]), mean_rate


def solution(mesh):
    n_tx, n_ty = mesh.shape["tx"], mesh.shape["ty"]
    side = math.isqrt(n_tx)
    return jax.shard_map(
        functools.partial(body, (side, side, n_ty // 2)),
        mesh=mesh,
        in_specs=(P(None, "tx", "ty"), P("tx", "ty"), P(None, ("tx", "ty"), None)),
        out_specs=(P(None, "tx", "ty"), P(None, "tx", "ty")),
        check_vma=False,
    )
```
